256 devices in a mesh: dp: 8 (over y, core), cent: 32 (over x, z).
Axes of the slice: x: 4, y: 4, z: 8, core: 2. Of those that a mesh axis runs over, the one named last changes fastest.
Arguments:
- passages: bfloat16 [32768, 768], P(('dp', 'cent')), may hold values from -10 to 10
- queries: bfloat16 [1024, 768], P(('dp', 'cent')), may hold values from -10 to 10
- init_centroids: float32 [8192, 768], P('cent'), may hold values from -12 to 12
- pattern: int32 [1024, 4], replicated, may hold values from 0 to 255, all different within a row
- positive_offset: int32 [1024], replicated, may hold values from 0 to 127
Outputs:
- centroids: float32 [8192, 768], P('cent')
- loss: float32 [1024], P(('dp', 'cent'))
The draws below stay inside these ranges and needn't reach their ends.
Inputs may be any that keep to these rules, and one draw needn't show every extreme that they name: `pattern`: each row names 4 different blocks.
All inputs are finite; a program needn't handle non-finite values.
Results may differ from the reference program's by a relative error of at most 0.0055.
Values may be sent and summed in bfloat16 or wider, within the bound.
A program may use at most 64 MiB of HBM per device.

```python
import jax
import jax.numpy as jnp
from jax import lax

D = 768
P_DEV = 128
BLOCK = 128
NB = 4
ITERS = 2
CENTERS = 8192
PASSAGES = 32768
QUERIES = 1024
NBLK = 256
N_CENT = 32


def draw_passages(key, part):
    drawn_rows = jnp.clip(jax.random.normal(jax.random.fold_in(key, 1), (PASSAGES, D), jnp.float32), -6.0, 6.0)
    return drawn_rows.astype(jnp.bfloat16)


def draw_queries(key, part):
    drawn_rows = jnp.clip(jax.random.normal(jax.random.fold_in(key, 3), (QUERIES, D), jnp.float32), -6.0, 6.0)
    return drawn_rows.astype(jnp.bfloat16)


def draw_init_centroids(key, part):
    drawn_rows = jnp.clip(jax.random.normal(jax.random.fold_in(key, 2), (CENTERS, D), jnp.float32), -6.0, 6.0)
    return drawn_rows


def with_ends(result, key, low, high):
    index_at = [jax.random.randint(jax.random.fold_in(key, axis), (), 0, length) for axis, length in enumerate(result.shape)]
    longest = result.shape.index(max(result.shape))
    next_to = index_at[:longest] + [(index_at[longest] + 1) % result.shape[longest]] + index_at[longest + 1:]
    return result.at[tuple(index_at)].set(low).at[tuple(next_to)].set(high)


def distinct(own_key, rows, number_of, top, lift):
    sequence = jax.random.permutation(jax.random.fold_in(own_key, 1), number_of)
    boost = sequence
    for power in range(3):
        boost = boost * boost // number_of
    boost = boost * lift // number_of
    tickets = jax.random.randint(jax.random.fold_in(own_key, 2), (rows, number_of), 0, 4096) + boost
    holders = jax.random.permutation(jax.random.fold_in(own_key, 3), rows)[jnp.arange(number_of) % rows]
    tickets = jnp.where(jnp.arange(rows)[:, None] == holders[None, :], 1 << 14, tickets)
    priority = tickets * number_of + jnp.arange(number_of)
    return lax.top_k(priority.astype(jnp.int32), top)[1].astype(jnp.int32)


def setup_inputs(seed: int = 0) -> dict:
    keys = jax.random.split(jax.random.key(seed), 6)
    passages = draw_passages(jax.random.fold_in(keys[5], 71), 0)
    queries = draw_queries(jax.random.fold_in(keys[5], 71), 0)
    init_centroids = draw_init_centroids(jax.random.fold_in(keys[5], 71), 0)
    pattern = distinct(keys[3], QUERIES, NBLK, NB, 256)
    positive_offset = with_ends(jax.random.randint(keys[4], (QUERIES,), 0, BLOCK), jax.random.fold_in(keys[4], 1), 0, BLOCK - 1).astype(jnp.int32)
    return dict(passages=passages, queries=queries, init_centroids=init_centroids, pattern=pattern, positive_offset=positive_offset)


sharpness = 0.05
sharpening_factor = 0.05
prior_weight = 1.0


def reference(passages, queries, init_centroids, pattern, positive_offset):
    cluster_means = init_centroids
    row_groups = passages.reshape(-1, P_DEV * N_CENT, D)
    for step_index in range(ITERS):
        centers_half = cluster_means.astype(jnp.bfloat16)
        cluster_center_norms = jnp.sum(cluster_means * cluster_means, axis=1)

        def group_terms(rows):
            unnormalized_log_odds = sharpness * (2.0 * jnp.dot(rows, centers_half.T, preferred_element_type=jnp.float32) - cluster_center_norms[None, :])
            resp = jax.nn.softmax(unnormalized_log_odds, axis=1)
            numer = jnp.dot(resp.astype(jnp.bfloat16).T, rows, preferred_element_type=jnp.float32)
            return numer, jnp.sum(resp, axis=0)

        numer_all, counts_all = lax.map(group_terms, row_groups)
        numer = jnp.sum(numer_all, axis=0)
        counts = jnp.sum(counts_all, axis=0)
        cluster_means = (numer + prior_weight * cluster_means) / (counts[:, None] + prior_weight)
    blocks = passages.reshape(NBLK, BLOCK, D)
    width = min(256, QUERIES)

    def query_terms(packed):
        question_tile_slice, picks, block_offsets = packed
        chosen_topic_label = blocks[picks]
        affinity_matrix = jnp.einsum("mz,mxdz->mxd", question_tile_slice.astype(jnp.float32), chosen_topic_label.astype(jnp.float32)) * sharpening_factor
        total = jax.scipy.special.logsumexp(affinity_matrix, axis=(1, 2))
        positive = jnp.take_along_axis(affinity_matrix[:, 0, :], block_offsets[:, None], axis=1)[:, 0]
        return total - positive

    losses = lax.map(query_terms, (queries.reshape(-1, width, D), pattern.reshape(-1, width, NB), positive_offset.reshape(-1, width)))
    return cluster_means, losses.reshape(QUERIES)
```

```python
import jax
import jax.numpy as jnp
from jax import lax
from jax.experimental import pallas as pl
from jax.experimental.pallas import tpu as pltpu
from jax.sharding import PartitionSpec as P

MESH = pl.DeviceIdType.MESH
BLOCK = 128
D = 768
NX, NZ, NY = 4, 8, 4
CENT = NX * NZ
DP = 2 * NY
KL = 256
QP = 64
W = D + 128
sharpness = 0.05
NEG = -1e30
F32 = jnp.float32
BF16 = jnp.bfloat16


def rcopy(src, dst, ss, rs, dev):
    return pltpu.make_async_remote_copy(
        src_ref=src, dst_ref=dst, send_sem=ss, recv_sem=rs, device_id=dev, device_id_type=MESH
    )


def kernel(
    p_ref, q_ref, c_ref, meta_ref, out_ref, loss_ref,
    G, E, S, CQ, C2, NB, acc, rb1, rb2, own, st_s, st_r, rs_r,
    qs, qr, qp_s, qp_r,
    g_ss, g_rs, q_ss, q_rs, st_ss, st_rs, rs_ss, rs_rs,
    n1_s, n2_ss, n2_rs, c_ss, c_rs, f_ss, f_rs, qp_ss, qp_rs, loc,
):
    dp = lax.axis_index("dp")
    me = lax.axis_index("cent")
    x, z = me // NZ, me % NZ
    y, core = dp // 2, dp % 2
    sib = (dp + 1 - 2 * core, me)

    def cdev(xx, zz):
        return (dp, xx * NZ + zz)

    barrier = pltpu.get_barrier_semaphore()

    def sig_cent(o, _):
        pl.semaphore_signal(barrier, inc=1, device_id=(dp, (me + o) % CENT), device_id_type=MESH)
        return 0

    lax.fori_loop(1, CENT, sig_cent, 0)

    def sig_dp(o, _):
        pl.semaphore_signal(barrier, inc=1, device_id=((dp + o) % DP, me), device_id_type=MESH)
        return 0

    lax.fori_loop(1, DP, sig_dp, 0)
    own_copy = pltpu.make_async_copy(p_ref, G.at[z, x], loc)
    own_copy.start()
    qs[...] = jnp.zeros_like(qs)
    qs[0:4, :] = q_ref[...].astype(F32)
    qr[dp] = qs[...]
    c0 = c_ref[...]
    CQ[0:KL, :] = c0.astype(BF16)
    NB[0] = jnp.broadcast_to(jnp.sum(c0 * c0, axis=1, keepdims=True), (KL, 128))
    pl.semaphore_wait(barrier, CENT + DP - 2)

    def q_copy(o, src):
        return rcopy(qs, qr.at[src], q_ss.at[o], q_rs.at[src], ((dp + o) % DP, me))

    def q_send(o, _):
        q_copy(o, dp).start()
        return 0

    lax.fori_loop(1, DP, q_send, 0)

    def g_copy(o, xs, zs):
        peer = (me + o) % CENT
        return rcopy(p_ref, G.at[zs, xs], g_ss.at[o], g_rs.at[zs, xs], (dp, peer))

    def g_send(o, _):
        g_copy(o, x, z).start()
        return 0

    lax.fori_loop(1, CENT, g_send, 0)

    def q_wait(o, _):
        q_copy(o, (dp + DP - o) % DP).wait_recv()
        return 0

    lax.fori_loop(1, DP, q_wait, 0)
    CQ[KL:KL + QP, :] = qr[...].reshape(QP, D).astype(BF16)
    own_copy.wait()

    def column(k):
        d = (k + 1) // 2
        sgn = 1 - 2 * (k % 2)
        return (z + NZ + sgn * d) % NZ

    def g_wait(zc, xc):
        g_copy(1, xc, zc).wait_recv()

    def st_copy(it, xc, zc, xs, zs):
        return rcopy(
            st_s.at[zc, xc], st_r.at[it, zs, xs], st_ss.at[zc, xc], st_rs.at[it, zs, xs], cdev(xc, zc)
        )

    def logits(it, zc, lhs):
        pc = G[zc].reshape(NX * BLOCK, D)
        dots = lax.dot_general(lhs, pc, (((1,), (1,)), ((), ())), preferred_element_type=F32)
        nb = NB[it]
        for xc in range(NX):
            lo = xc * BLOCK
            ll = sharpness * (2.0 * dots[0:KL, lo:lo + BLOCK] - nb)
            m = jnp.max(ll, axis=0, keepdims=True)
            e = jnp.exp(ll - m)
            s = jnp.sum(e, axis=0, keepdims=True)
            E[zc, :, lo:lo + BLOCK] = e
            st_s[zc, xc, 0:1, :] = m
            st_s[zc, xc, 1:2, :] = s
        if it == 0:
            S[zc] = dots[KL:KL + QP, :] * sharpness

    def softmax_pass(it, lhs_of):
        if it == 0:
            for i in range(1, NX):
                g_wait(z, (x + i) % NX)
        logits(it, z, lhs_of())
        st_r[it, z, x] = st_s[z, x]
        for i in range(1, NX):
            st_copy(it, (x + i) % NX, z, x, z).start()

        def col_step(k, _):
            zc = column(k)
            if it == 0:
                for xc in range(NX):
                    g_wait(zc, xc)
            logits(it, zc, lhs_of())
            for xc in range(NX):
                st_copy(it, xc, zc, x, z).start()
            return 0

        lax.fori_loop(1, NZ, col_step, 0)

    def rs_copy(it, o, xo, zo):
        peer = (me + o) % CENT
        return rcopy(
            rs_r.at[it, z, x], rs_r.at[it, zo, xo], rs_ss.at[it, o], rs_rs.at[it, zo, xo], (dp, peer)
        )

    def owner_combine(it):
        def w(o, _):
            src = (me + o) % CENT
            st_copy(it, x, z, src // NZ, src % NZ).wait_recv()
            return 0

        lax.fori_loop(1, CENT, w, 0)
        m = st_r[it, :, :, 0:1, :].reshape(CENT, 1, BLOCK)
        s = st_r[it, :, :, 1:2, :].reshape(CENT, 1, BLOCK)
        top = jnp.max(m, axis=0)
        tot = jnp.sum(s * jnp.exp(m - top[None]), axis=0)
        rs_r[it, z, x, 0:1, :] = top
        rs_r[it, z, x, 1:2, :] = 1.0 / tot

        def snd(o, _):
            rs_copy(it, o, x, z).start()
            return 0

        lax.fori_loop(1, CENT, snd, 0)

    def query_post():
        meta = meta_ref[...]
        pats = [jnp.broadcast_to(meta[:, i:i + 1], (QP, BLOCK)) for i in range(4)]
        off = jnp.broadcast_to(meta[:, 4:5], (QP, BLOCK))
        lane = lax.broadcasted_iota(jnp.int32, (QP, BLOCK), 1)

        def allow_of(b):
            return (pats[0] == b) | (pats[1] == b) | (pats[2] == b) | (pats[3] == b)

        def p1(zc, mx):
            for xc in range(NX):
                b = dp * CENT + xc * NZ + zc
                sv = S[zc, :, xc * BLOCK:(xc + 1) * BLOCK]
                mx = jnp.maximum(mx, jnp.where(allow_of(b), sv, NEG))
            return mx

        mx = lax.fori_loop(0, NZ, p1, jnp.full((QP, BLOCK), NEG, F32))
        mrow = jnp.max(mx, axis=1, keepdims=True)
        mb = jnp.broadcast_to(mrow, (QP, BLOCK))

        def p2(zc, carry):
            tot, pos = carry
            for xc in range(NX):
                b = dp * CENT + xc * NZ + zc
                sv = S[zc, :, xc * BLOCK:(xc + 1) * BLOCK]
                tot = tot + jnp.where(allow_of(b), jnp.exp(sv - mb), 0.0)
                pos = pos + jnp.where((pats[0] == b) & (lane == off), sv, 0.0)
            return tot, pos

        zero = jnp.zeros((QP, BLOCK), F32)
        tot, pos = lax.fori_loop(0, NZ, p2, (zero, zero))
        trow = jnp.broadcast_to(jnp.sum(tot, axis=1, keepdims=True), (QP, BLOCK))
        prow = jnp.broadcast_to(jnp.sum(pos, axis=1, keepdims=True), (QP, BLOCK))
        packed = jnp.where(lane == 0, mb, jnp.where(lane == 1, trow, prow))
        qp_s[...] = packed.reshape(DP, 8, BLOCK)
        qp_r[dp] = qp_s[dp]

        def snd(o, _):
            qp_copy(o, (dp + o) % DP, dp).start()
            return 0

        lax.fori_loop(1, DP, snd, 0)

    def qp_copy(o, dst, src):
        return rcopy(qp_s.at[dst], qp_r.at[src], qp_ss.at[o], qp_rs.at[src], (dst, me))

    def query_finish():
        def w(o, _):
            qp_copy(o, (dp + o) % DP, (dp + o) % DP).wait_recv()
            return 0

        lax.fori_loop(1, DP, w, 0)
        m = qp_r[:, :, 0:1]
        t = qp_r[:, :, 1:2]
        p = qp_r[:, :, 2:3]
        top = jnp.max(m, axis=0)
        tot = jnp.sum(t * jnp.exp(m - top[None]), axis=0)
        ps = jnp.sum(p, axis=0)
        loss_ref[...] = jnp.broadcast_to(jnp.log(tot) + top - ps, (8, BLOCK))

        def ws(o, _):
            qp_copy(o, (dp + o) % DP, dp).wait_send()
            return 0

        lax.fori_loop(1, DP, ws, 0)

    def numer_pass(it):
        def w(o, _):
            src = (me + o) % CENT
            rs_copy(it, o, src // NZ, src % NZ).wait_recv()
            return 0

        lax.fori_loop(1, CENT, w, 0)
        acc[...] = jnp.zeros_like(acc)

        def col(zc, _):
            cnt = acc[:, D:W]
            parts = []
            for xc in range(NX):
                g = jnp.exp(st_s[zc, xc, 0:1, :] - rs_r[it, zc, xc, 0:1, :]) * rs_r[it, zc, xc, 1:2, :]
                r = E[zc, :, xc * BLOCK:(xc + 1) * BLOCK] * g
                cnt = cnt + r
                parts.append(r.astype(BF16))
            acc[:, D:W] = cnt
            r_all = jnp.concatenate(parts, axis=1)
            acc[:, 0:D] += jnp.dot(r_all, G[zc].reshape(NX * BLOCK, D), preferred_element_type=F32)
            return 0

        lax.fori_loop(0, NZ, col, 0)

        def ws(o, _):
            dst = (me + o) % CENT
            st_copy(it, dst // NZ, dst % NZ, x, z).wait_send()
            rs_copy(it, o, x, z).wait_send()
            return 0

        lax.fori_loop(1, CENT, ws, 0)

    half = pl.multiple_of(core * 128, 128)
    other = pl.multiple_of(128 - core * 128, 128)
    myrow = pl.multiple_of(core * 128 + y * 32, 32)

    def reduce_dp(it):
        c1 = rcopy(acc.at[pl.ds(other, 128)], rb1.at[it], n1_s.at[it, 0], n1_s.at[it, 1], sib)
        c1.start()
        c1.wait_recv()
        acc[pl.ds(half, 128), :] += rb1[it]
        cs = []
        for i in range(1, NY):
            yp = (y + i) % NY
            rows = pl.ds(pl.multiple_of(core * 128 + yp * 32, 32), 32)
            c = rcopy(acc.at[rows], rb2.at[it, i - 1], n2_ss.at[it, i - 1], n2_rs.at[it, i - 1], (yp * 2 + core, me))
            c.start()
            cs.append(c)
        tot = acc[pl.ds(myrow, 32), :]
        for i in range(NY - 1):
            cs[i].wait_recv()
            tot = tot + rb2[it, i]
        c1.wait_send()
        for c in cs:
            c.wait_send()
        counts = jnp.sum(tot[:, D:W], axis=1, keepdims=True)
        cold = c_ref[pl.ds(myrow, 32), :] if it == 0 else own[...]
        return (tot[:, 0:D] + cold) / (counts + 1.0)

    def spread(arr, ss, rs, k):
        rows = arr.at[pl.ds(myrow, 32)]
        cs = []
        for i in range(1, NY):
            yp = (y + i) % NY
            cs.append(rcopy(rows, rows, ss.at[k, i - 1], rs.at[k, i - 1], (yp * 2 + core, me)))
        cs.append(rcopy(rows, rows, ss.at[k, 3], rs.at[k, 3], sib))
        return cs

    def all_gather_rows(arrs, ss, rs):
        groups = [spread(a, ss, rs, k) for k, a in enumerate(arrs)]
        for i in range(NY):
            for g in groups:
                g[i].start()
        fw = []
        for i in range(1, NY):
            ysrc = (y + NY - i) % NY
            rows = pl.ds(pl.multiple_of(core * 128 + ysrc * 32, 32), 32)
            for k, a in enumerate(arrs):
                groups[k][i - 1].wait_recv()
                c = rcopy(a.at[rows], a.at[rows], ss.at[k, 3 + i], rs.at[k, 3 + i], sib)
                c.start()
                fw.append(c)
        for g in groups:
            g[3].wait_recv()
        for c in fw:
            c.wait_recv()
        for g in groups:
            for c in g:
                c.wait_send()
        for c in fw:
            c.wait_send()

    softmax_pass(0, lambda: CQ[...])
    owner_combine(0)
    query_post()
    numer_pass(0)
    newc = reduce_dp(0)
    own[...] = newc
    C2[pl.ds(myrow, 32), :] = newc.astype(BF16)
    NB[1, pl.ds(myrow, 32), :] = jnp.broadcast_to(jnp.sum(newc * newc, axis=1, keepdims=True), (32, 128))
    all_gather_rows([C2, NB.at[1]], c_ss, c_rs)

    softmax_pass(1, lambda: C2[...])
    owner_combine(1)
    query_finish()
    numer_pass(1)
    out_ref[pl.ds(myrow, 32), :] = reduce_dp(1)
    all_gather_rows([out_ref], f_ss, f_rs)

    def ws(o, _):
        g_copy(o, x, z).wait_send()
        return 0

    lax.fori_loop(1, CENT, ws, 0)

    def wsq(o, _):
        q_copy(o, dp).wait_send()
        return 0

    lax.fori_loop(1, DP, wsq, 0)


def on_device(passages, queries, init_centroids, pattern, positive_offset):
    me = lax.axis_index("cent")
    meta = jnp.concatenate([pattern, positive_offset[:, None]], axis=1).reshape(DP, CENT, 4, 5)
    meta = lax.dynamic_index_in_dim(meta, me, 1, keepdims=False)
    meta = jnp.pad(meta, ((0, 0), (0, 4), (0, 123)), constant_values=-1).reshape(QP, 128)
    vm = pl.BlockSpec(memory_space=pltpu.VMEM)
    dma = pltpu.SemaphoreType.DMA
    centroids, loss = pl.pallas_call(
        kernel,
        out_shape=(jax.ShapeDtypeStruct((KL, D), F32), jax.ShapeDtypeStruct((8, 128), F32)),
        in_specs=[vm] * 4,
        out_specs=(vm, vm),
        scratch_shapes=[
            pltpu.VMEM((NZ, NX, BLOCK, D), BF16),
            pltpu.VMEM((NZ, KL, NX * BLOCK), F32),
            pltpu.VMEM((NZ, QP, NX * BLOCK), F32),
            pltpu.VMEM((KL + QP, D), BF16),
            pltpu.VMEM((KL, D), BF16),
            pltpu.VMEM((2, KL, 128), F32),
            pltpu.VMEM((KL, W), F32),
            pltpu.VMEM((2, 128, W), F32),
            pltpu.VMEM((2, NY - 1, 32, W), F32),
            pltpu.VMEM((32, D), F32),
            pltpu.VMEM((NZ, NX, 2, 128), F32),
            pltpu.VMEM((2, NZ, NX, 2, 128), F32),
            pltpu.VMEM((2, NZ, NX, 2, 128), F32),
            pltpu.VMEM((8, D), F32),
            pltpu.VMEM((DP, 8, D), F32),
            pltpu.VMEM((DP, 8, 128), F32),
            pltpu.VMEM((DP, 8, 128), F32),
            dma((CENT,)), dma((NZ, NX)),
            dma((DP,)), dma((DP,)),
            dma((NZ, NX)), dma((2, NZ, NX)),
            dma((2, CENT)), dma((2, NZ, NX)),
            dma((2, 2)), dma((2, 3)), dma((2, 3)),
            dma((2, 8)), dma((2, 8)),
            dma((1, 8)), dma((1, 8)),
            dma((DP,)), dma((DP,)),
            dma,
        ],
        compiler_params=pltpu.CompilerParams(
            collective_id=0, has_side_effects=True, vmem_limit_bytes=40 * 1024 * 1024
        ),
    )(passages, queries, init_centroids, meta)
    return centroids, loss[:4, 0]


def solution(mesh):
    placed = (P(("dp", "cent"), None), P(("dp", "cent"), None), P("cent", None), P(), P())
    return jax.shard_map(
        on_device,
        mesh=mesh,
        in_specs=placed,
        out_specs=(P("cent", None), P(("dp", "cent"))),
        check_vma=False,
    )
```

```python
import jax
import jax.numpy as jnp
from jax import lax
from jax.experimental import pallas as pl
from jax.experimental.pallas import tpu as pltpu
from jax.sharding import PartitionSpec as P

MESH = pl.DeviceIdType.MESH
BLOCK = 128
D = 768
NX, NZ, NY = 4, 8, 4
CENT = NX * NZ
DP = 2 * NY
KL = 256
QP = 64
W = D + 128
sharpness = 0.05
NEG = -1e30
RA, RB = 80, 48
HD = D // 2
STOP = 99
F32 = jnp.float32
BF16 = jnp.bfloat16


def rcopy(src, dst, ss, rs, dev):
    return pltpu.make_async_remote_copy(
        src_ref=src, dst_ref=dst, send_sem=ss, recv_sem=rs, device_id=dev, device_id_type=MESH
    )


def kernel(
    p_ref, q_ref, c_ref, meta_ref, out_ref, loss_ref,
    G, E, S, CQ, C2, NB, acc, rb1, rb2, own, st_s, st_r, rs_r,
    qs, qr, qp_s, qp_r,
    az_ss, az_rs, bz_ss, bz_rs, ax_ss, ax_rs, bx_ss, bx_rs, q_ss, q_rs, st_ss, st_rs, rs_ss, rs_rs,
    n1_s, n2_ss, n2_rs, c_ss, c_rs, f_ss, f_rs, qp_ss, qp_rs,
):
    dp = lax.axis_index("dp")
    me = lax.axis_index("cent")
    x, z = me // NZ, me % NZ
    y, core = dp // 2, dp % 2
    sib = (dp + 1 - 2 * core, me)

    def cdev(xx, zz):
        return (dp, xx * NZ + zz)

    barrier = pltpu.get_barrier_semaphore()

    def sig_cent(o, _):
        pl.semaphore_signal(barrier, inc=1, device_id=(dp, (me + o) % CENT), device_id_type=MESH)
        return 0

    lax.fori_loop(1, CENT, sig_cent, 0)

    def sig_dp(o, _):
        pl.semaphore_signal(barrier, inc=1, device_id=((dp + o) % DP, me), device_id_type=MESH)
        return 0

    lax.fori_loop(1, DP, sig_dp, 0)
    G[z, x] = p_ref[...]
    qs[...] = jnp.zeros_like(qs)
    qs[0:4, :] = q_ref[...].astype(F32)
    qr[dp] = qs[...]
    c0 = c_ref[...]
    CQ[0:KL, :] = c0.astype(BF16)
    NB[0] = jnp.broadcast_to(jnp.sum(c0 * c0, axis=1, keepdims=True), (KL, 128))
    pl.semaphore_wait(barrier, CENT + DP - 2)

    def q_copy(o, src):
        return rcopy(qs, qr.at[src], q_ss.at[o], q_rs.at[src], ((dp + o) % DP, me))

    def q_send(o, _):
        q_copy(o, dp).start()
        return 0

    lax.fori_loop(1, DP, q_send, 0)

    def zdev(step):
        return (dp, x * NZ + (z + NZ + step) % NZ)

    def xdev(step):
        return (dp, ((x + NX + step) % NX) * NZ + z)

    STEP = (1, -1)

    def a_z(zs, side, part=None):
        lo, n = (0, D) if part is None else (part * HD, HD)
        ref = G.at[zs, x, pl.ds(0, RA), pl.ds(lo, n)]
        return rcopy(ref, ref, az_ss.at[zs, side], az_rs.at[zs if part != 1 else NZ], zdev(STEP[side]))

    def b_z(zs, side, part=None):
        lo, n = (0, NX) if part is None else (part * (NX // 2), NX // 2)
        ref = G.at[zs, pl.ds(lo, n), pl.ds(RA, RB)]
        return rcopy(ref, ref, bz_ss.at[zs, side], bz_rs.at[zs if part != 1 else NZ], zdev(STEP[side]))

    def a_x(zs, xs, side):
        ref = G.at[zs, xs, pl.ds(0, RA)]
        return rcopy(ref, ref, ax_ss.at[zs, side], ax_rs.at[zs, side], xdev(STEP[side]))

    def a_x2(zs, xs, side):
        ref = G.at[zs, xs, pl.ds(0, RA), pl.ds(side * HD, HD)]
        return rcopy(ref, ref, ax_ss.at[zs, 2 + side], ax_rs.at[zs, 2 + side], xdev(STEP[side]))

    def b_x(xs, side):
        ref = G.at[z, xs, pl.ds(RA, RB)]
        return rcopy(ref, ref, bx_ss.at[side], bx_rs.at[side], xdev(STEP[side]))

    def b_x2(xs, side):
        ref = G.at[z, xs, pl.ds(RA, RB), pl.ds(side * HD, HD)]
        return rcopy(ref, ref, bx_ss.at[2 + side], bx_rs.at[2 + side], xdev(STEP[side]))

    def xfrom(side, n=1):
        return (x + NX - n * STEP[side]) % NX

    def zfrom(side, n):
        return (z + NZ - n * STEP[side]) % NZ

    def send_ax(zs):
        for side in range(2):
            a_x(zs, x, side).start()

    def hop_ax(zs):
        for side in range(2):
            a_x(zs, xfrom(side), side).wait_recv()
            a_x2(zs, xfrom(side), side).start()

    def end_ax(zs):
        for side in range(2):
            a_x2(zs, xfrom(side, 2), side).wait_recv()

    def take_a(d):
        for side in range(2):
            zs = zfrom(side, d)
            if d < 4:
                a_z(zs, side).wait_recv()
                a_z(zs, side, None if d < 3 else side).start()
                send_ax(zs)
            else:
                a_z(zs, side, side).wait_recv()
        if d == 4:
            send_ax(zfrom(0, 4))

    def take_b(d):
        for side in range(2):
            zs = zfrom(side, d)
            if d < 4:
                b_z(zs, side).wait_recv()
                b_z(zs, side, None if d < 3 else side).start()
            else:
                b_z(zs, side, side).wait_recv()

    def gather(compute):
        for side in range(2):
            a_z(z, side).start()
        for side in range(2):
            b_x(x, side).start()
        send_ax(z)
        early()
        for side in range(2):
            b_x(xfrom(side), side).wait_recv()
            b_x2(xfrom(side), side).start()
        for side in range(2):
            b_x2(xfrom(side, 2), side).wait_recv()
        for side in range(2):
            b_z(z, side).start()
        take_a(1)
        hop_ax(z)
        end_ax(z)
        compute(0)
        take_b(1)
        for side in range(2):
            hop_ax(zfrom(side, 1))
        for d in range(2, 5):
            take_a(d)
            for side in range(2):
                end_ax(zfrom(side, d - 1))
            compute(d - 1)
            take_b(d)
            for side in range(2 if d < 4 else 1):
                hop_ax(zfrom(side, d))
        end_ax(zfrom(0, 4))
        compute(4)

    def gather_drain():
        for side in range(2):
            b_x(x, side).wait_send()
            b_x2(xfrom(side), side).wait_send()
            for d in range(4):
                zs = zfrom(side, d)
                a_z(zs, side, None if d < 3 else side).wait_send()
                b_z(zs, side, None if d < 3 else side).wait_send()

        def w(zs, _):
            for side in range(2):
                a_x(zs, x, side).wait_send()
                a_x2(zs, xfrom(side), side).wait_send()
            return 0

        lax.fori_loop(0, NZ, w, 0)

    def q_wait(o, _):
        q_copy(o, (dp + DP - o) % DP).wait_recv()
        return 0

    def early():
        lax.fori_loop(1, DP, q_wait, 0)
        CQ[KL:KL + QP, :] = qr[...].reshape(QP, D).astype(BF16)

    def column(k):
        d = (k + 1) // 2
        sgn = 1 - 2 * (k % 2)
        return (z + NZ + sgn * d) % NZ

    def st_copy(it, xc, zc, xs, zs):
        return rcopy(
            st_s.at[zc, xc], st_r.at[it, zs, xs], st_ss.at[zc, xc], st_rs.at[it, zs, xs], cdev(xc, zc)
        )

    def logits(it, zc, lhs):
        pc = G[zc].reshape(NX * BLOCK, D)
        dots = lax.dot_general(lhs, pc, (((1,), (1,)), ((), ())), preferred_element_type=F32)
        nb = NB[it]
        for xc in range(NX):
            lo = xc * BLOCK
            ll = sharpness * (2.0 * dots[0:KL, lo:lo + BLOCK] - nb)
            m = jnp.max(ll, axis=0, keepdims=True)
            e = jnp.exp(ll - m)
            s = jnp.sum(e, axis=0, keepdims=True)
            E[zc, :, lo:lo + BLOCK] = e
            st_s[zc, xc, 0:1, :] = m
            st_s[zc, xc, 1:2, :] = s
        if it == 0:
            S[zc] = dots[KL:KL + QP, :] * sharpness

    def own_column(it, lhs):
        logits(it, z, lhs)
        st_r[it, z, x] = st_s[z, x]
        for i in range(1, NX):
            st_copy(it, (x + i) % NX, z, x, z).start()

    def other_column(it, zc, lhs):
        logits(it, zc, lhs)
        for xc in range(NX):
            st_copy(it, xc, zc, x, z).start()

    def softmax_first():
        def compute(d):
            if d == 0:
                own_column(0, CQ[...])
            elif d == 4:
                other_column(0, zfrom(0, 4), CQ[...])
            else:
                def side_step(i, _):
                    other_column(0, (z + NZ + (2 * i - 1) * d) % NZ, CQ[...])
                    return 0

                lax.fori_loop(0, 2, side_step, 0)

        gather(compute)

    def softmax_second():
        own_column(1, C2[...])

        def col_step(k, _):
            other_column(1, column(k), C2[...])
            return 0

        lax.fori_loop(1, NZ, col_step, 0)

    def rs_copy(it, o, xo, zo):
        peer = (me + o) % CENT
        return rcopy(
            rs_r.at[it, z, x], rs_r.at[it, zo, xo], rs_ss.at[it, o], rs_rs.at[it, zo, xo], (dp, peer)
        )

    def owner_combine(it):
        def w(o, _):
            src = (me + o) % CENT
            st_copy(it, x, z, src // NZ, src % NZ).wait_recv()
            return 0

        lax.fori_loop(1, CENT, w, 0)
        m = st_r[it, :, :, 0:1, :].reshape(CENT, 1, BLOCK)
        s = st_r[it, :, :, 1:2, :].reshape(CENT, 1, BLOCK)
        top = jnp.max(m, axis=0)
        tot = jnp.sum(s * jnp.exp(m - top[None]), axis=0)
        rs_r[it, z, x, 0:1, :] = top
        rs_r[it, z, x, 1:2, :] = 1.0 / tot

        def snd(o, _):
            rs_copy(it, o, x, z).start()
            return 0

        lax.fori_loop(1, CENT, snd, 0)

    def query_post():
        meta = meta_ref[...]
        pats = [jnp.broadcast_to(meta[:, i:i + 1], (QP, BLOCK)) for i in range(4)]
        off = jnp.broadcast_to(meta[:, 4:5], (QP, BLOCK))
        lane = lax.broadcasted_iota(jnp.int32, (QP, BLOCK), 1)

        def allow_of(b):
            return (pats[0] == b) | (pats[1] == b) | (pats[2] == b) | (pats[3] == b)

        def p1(zc, mx):
            for xc in range(NX):
                b = dp * CENT + xc * NZ + zc
                sv = S[zc, :, xc * BLOCK:(xc + 1) * BLOCK]
                mx = jnp.maximum(mx, jnp.where(allow_of(b), sv, NEG))
            return mx

        mx = lax.fori_loop(0, NZ, p1, jnp.full((QP, BLOCK), NEG, F32))
        mrow = jnp.max(mx, axis=1, keepdims=True)
        mb = jnp.broadcast_to(mrow, (QP, BLOCK))

        def p2(zc, carry):
            tot, pos = carry
            for xc in range(NX):
                b = dp * CENT + xc * NZ + zc
                sv = S[zc, :, xc * BLOCK:(xc + 1) * BLOCK]
                tot = tot + jnp.where(allow_of(b), jnp.exp(sv - mb), 0.0)
                pos = pos + jnp.where((pats[0] == b) & (lane == off), sv, 0.0)
            return tot, pos

        zero = jnp.zeros((QP, BLOCK), F32)
        tot, pos = lax.fori_loop(0, NZ, p2, (zero, zero))
        trow = jnp.broadcast_to(jnp.sum(tot, axis=1, keepdims=True), (QP, BLOCK))
        prow = jnp.broadcast_to(jnp.sum(pos, axis=1, keepdims=True), (QP, BLOCK))
        packed = jnp.where(lane == 0, mb, jnp.where(lane == 1, trow, prow))
        qp_s[...] = packed.reshape(DP, 8, BLOCK)
        qp_r[dp] = qp_s[dp]

        def snd(o, _):
            qp_copy(o, (dp + o) % DP, dp).start()
            return 0

        lax.fori_loop(1, DP, snd, 0)

    def qp_copy(o, dst, src):
        return rcopy(qp_s.at[dst], qp_r.at[src], qp_ss.at[o], qp_rs.at[src], (dst, me))

    def query_finish():
        def w(o, _):
            qp_copy(o, (dp + o) % DP, (dp + o) % DP).wait_recv()
            return 0

        lax.fori_loop(1, DP, w, 0)
        m = qp_r[:, :, 0:1]
        t = qp_r[:, :, 1:2]
        p = qp_r[:, :, 2:3]
        top = jnp.max(m, axis=0)
        tot = jnp.sum(t * jnp.exp(m - top[None]), axis=0)
        ps = jnp.sum(p, axis=0)
        loss_ref[...] = jnp.broadcast_to(jnp.log(tot) + top - ps, (8, BLOCK))

        def ws(o, _):
            qp_copy(o, (dp + o) % DP, dp).wait_send()
            return 0

        lax.fori_loop(1, DP, ws, 0)

    def numer_pass(it):
        def w(o, _):
            src = (me + o) % CENT
            rs_copy(it, o, src // NZ, src % NZ).wait_recv()
            return 0

        lax.fori_loop(1, CENT, w, 0)
        acc[...] = jnp.zeros_like(acc)

        def col(zc, _):
            cnt = acc[:, D:W]
            parts = []
            for xc in range(NX):
                g = jnp.exp(st_s[zc, xc, 0:1, :] - rs_r[it, zc, xc, 0:1, :]) * rs_r[it, zc, xc, 1:2, :]
                r = E[zc, :, xc * BLOCK:(xc + 1) * BLOCK] * g
                cnt = cnt + r
                parts.append(r.astype(BF16))
            acc[:, D:W] = cnt
            r_all = jnp.concatenate(parts, axis=1)
            acc[:, 0:D] += jnp.dot(r_all, G[zc].reshape(NX * BLOCK, D), preferred_element_type=F32)
            return 0

        lax.fori_loop(0, NZ, col, 0)

        def ws(o, _):
            dst = (me + o) % CENT
            st_copy(it, dst // NZ, dst % NZ, x, z).wait_send()
            rs_copy(it, o, x, z).wait_send()
            return 0

        lax.fori_loop(1, CENT, ws, 0)

    half = pl.multiple_of(core * 128, 128)
    other = pl.multiple_of(128 - core * 128, 128)
    myrow = pl.multiple_of(core * 128 + y * 32, 32)

    def reduce_dp(it):
        c1 = rcopy(acc.at[pl.ds(other, 128)], rb1.at[it], n1_s.at[it, 0], n1_s.at[it, 1], sib)
        c1.start()
        c1.wait_recv()
        acc[pl.ds(half, 128), :] += rb1[it]
        cs = []
        for i in range(1, NY):
            yp = (y + i) % NY
            rows = pl.ds(pl.multiple_of(core * 128 + yp * 32, 32), 32)
            c = rcopy(acc.at[rows], rb2.at[it, i - 1], n2_ss.at[it, i - 1], n2_rs.at[it, i - 1], (yp * 2 + core, me))
            c.start()
            cs.append(c)
        tot = acc[pl.ds(myrow, 32), :]
        for i in range(NY - 1):
            cs[i].wait_recv()
            tot = tot + rb2[it, i]
        c1.wait_send()
        for c in cs:
            c.wait_send()
        counts = jnp.sum(tot[:, D:W], axis=1, keepdims=True)
        cold = c_ref[pl.ds(myrow, 32), :] if it == 0 else own[...]
        return (tot[:, 0:D] + cold) / (counts + 1.0)

    def spread(arr, ss, rs, k):
        rows = arr.at[pl.ds(myrow, 32)]
        cs = []
        for i in range(1, NY):
            yp = (y + i) % NY
            cs.append(rcopy(rows, rows, ss.at[k, i - 1], rs.at[k, i - 1], (yp * 2 + core, me)))
        cs.append(rcopy(rows, rows, ss.at[k, 3], rs.at[k, 3], sib))
        return cs

    def all_gather_rows(arrs, ss, rs):
        groups = [spread(a, ss, rs, k) for k, a in enumerate(arrs)]
        for i in range(NY):
            for g in groups:
                g[i].start()
        fw = []
        for i in range(1, NY):
            ysrc = (y + NY - i) % NY
            rows = pl.ds(pl.multiple_of(core * 128 + ysrc * 32, 32), 32)
            for k, a in enumerate(arrs):
                groups[k][i - 1].wait_recv()
                c = rcopy(a.at[rows], a.at[rows], ss.at[k, 3 + i], rs.at[k, 3 + i], sib)
                c.start()
                fw.append(c)
        for g in groups:
            g[3].wait_recv()
        for c in fw:
            c.wait_recv()
        for g in groups:
            for c in g:
                c.wait_send()
        for c in fw:
            c.wait_send()

    def finish():
        if STOP >= 0:
            gather_drain()

        def wsq(o, _):
            q_copy(o, dp).wait_send()
            return 0

        lax.fori_loop(1, DP, wsq, 0)
        if STOP < 90:
            out_ref[...] = jnp.zeros_like(out_ref)
            loss_ref[...] = jnp.zeros_like(loss_ref)

    def drain(it):
        def ws(o, _):
            dst = (me + o) % CENT
            st_copy(it, dst // NZ, dst % NZ, x, z).wait_send()
            rs_copy(it, o, x, z).wait_send()
            rs_copy(it, o, dst // NZ, dst % NZ).wait_recv()
            return 0

        lax.fori_loop(1, CENT, ws, 0)

    if STOP == 0:
        gather(lambda d: None)
        return finish()
    if STOP == -1:
        early()
        return finish()
    softmax_first()
    owner_combine(0)
    if STOP == 1:
        drain(0)
        return finish()
    query_post()
    if STOP == 2:
        drain(0)
        query_finish()
        return finish()
    numer_pass(0)
    if STOP == 3:
        query_finish()
        return finish()
    newc = reduce_dp(0)
    own[...] = newc
    C2[pl.ds(myrow, 32), :] = newc.astype(BF16)
    NB[1, pl.ds(myrow, 32), :] = jnp.broadcast_to(jnp.sum(newc * newc, axis=1, keepdims=True), (32, 128))
    if STOP == 4:
        query_finish()
        return finish()
    all_gather_rows([C2, NB.at[1]], c_ss, c_rs)
    if STOP == 5:
        query_finish()
        return finish()

    softmax_second()
    owner_combine(1)
    query_finish()
    if STOP == 6:
        drain(1)
        return finish()
    numer_pass(1)
    if STOP == 7:
        return finish()
    out_ref[pl.ds(myrow, 32), :] = reduce_dp(1)
    if STOP == 8:
        return finish()
    all_gather_rows([out_ref], f_ss, f_rs)
    finish()


def on_device(passages, queries, init_centroids, pattern, positive_offset):
    me = lax.axis_index("cent")
    meta = jnp.concatenate([pattern, positive_offset[:, None]], axis=1).reshape(DP, CENT, 4, 5)
    meta = lax.dynamic_index_in_dim(meta, me, 1, keepdims=False)
    meta = jnp.pad(meta, ((0, 0), (0, 4), (0, 123)), constant_values=-1).reshape(QP, 128)
    vm = pl.BlockSpec(memory_space=pltpu.VMEM)
    dma = pltpu.SemaphoreType.DMA
    centroids, loss = pl.pallas_call(
        kernel,
        out_shape=(jax.ShapeDtypeStruct((KL, D), F32), jax.ShapeDtypeStruct((8, 128), F32)),
        in_specs=[vm] * 4,
        out_specs=(vm, vm),
        scratch_shapes=[
            pltpu.VMEM((NZ, NX, BLOCK, D), BF16),
            pltpu.VMEM((NZ, KL, NX * BLOCK), F32),
            pltpu.VMEM((NZ, QP, NX * BLOCK), F32),
            pltpu.VMEM((KL + QP, D), BF16),
            pltpu.VMEM((KL, D), BF16),
            pltpu.VMEM((2, KL, 128), F32),
            pltpu.VMEM((KL, W), F32),
            pltpu.VMEM((2, 128, W), F32),
            pltpu.VMEM((2, NY - 1, 32, W), F32),
            pltpu.VMEM((32, D), F32),
            pltpu.VMEM((NZ, NX, 2, 128), F32),
            pltpu.VMEM((2, NZ, NX, 2, 128), F32),
            pltpu.VMEM((2, NZ, NX, 2, 128), F32),
            pltpu.VMEM((8, D), F32),
            pltpu.VMEM((DP, 8, D), F32),
            pltpu.VMEM((DP, 8, 128), F32),
            pltpu.VMEM((DP, 8, 128), F32),
            dma((NZ, 2)), dma((NZ + 1,)), dma((NZ, 2)), dma((NZ + 1,)),
            dma((NZ, 4)), dma((NZ, 4)), dma((4,)), dma((4,)),
            dma((DP,)), dma((DP,)),
            dma((NZ, NX)), dma((2, NZ, NX)),
            dma((2, CENT)), dma((2, NZ, NX)),
            dma((2, 2)), dma((2, 3)), dma((2, 3)),
            dma((2, 8)), dma((2, 8)),
            dma((1, 8)), dma((1, 8)),
            dma((DP,)), dma((DP,)),
        ],
        compiler_params=pltpu.CompilerParams(
            collective_id=0, has_side_effects=True, vmem_limit_bytes=40 * 1024 * 1024
        ),
    )(passages, queries, init_centroids, meta)
    return centroids, loss[:4, 0]


def solution(mesh):
    placed = (P(("dp", "cent"), None), P(("dp", "cent"), None), P("cent", None), P(), P())
    return jax.shard_map(
        on_device,
        mesh=mesh,
        in_specs=placed,
        out_specs=(P("cent", None), P(("dp", "cent"))),
        check_vma=False,
    )
```

```python
import jax
import jax.numpy as jnp
from jax import lax
from jax.experimental import pallas as pl
from jax.experimental.pallas import tpu as pltpu
from jax.sharding import PartitionSpec as P

MESH = pl.DeviceIdType.MESH
BLOCK = 128
D = 768
HD = 384
NX, NZ, NY = 4, 8, 4
CENT = NX * NZ
DP = 2 * NY
KL = 256
QP = 64
W = D + 128
CH = 2
RC = KL // CH
RH = RC // 2
RQ = RH // NY
sharpness = 0.05
NEG = -1e30
STOP = 99
RA = 80
RB = 128 - RA
NARROW = (True, False)
F32 = jnp.float32
BF16 = jnp.bfloat16


def rcopy(src, dst, ss, rs, dev):
    return pltpu.make_async_remote_copy(
        src_ref=src, dst_ref=dst, send_sem=ss, recv_sem=rs, device_id=dev, device_id_type=MESH
    )


def three(v, rows):
    lane = lax.broadcasted_iota(jnp.int32, (rows, 128), 1)
    v = jnp.broadcast_to(v, (rows, 128))
    hi = v.astype(BF16).astype(F32)
    mid = (v - hi).astype(BF16).astype(F32)
    lo = v - hi - mid
    return jnp.where(lane == 0, hi, jnp.where(lane == 1, mid, jnp.where(lane == 2, lo, 0.0))).astype(BF16)


def kernel(
    p_ref, q_ref, c_ref, pat_ref, off_ref, out_ref, loss_ref,
    G, E, S, CQ, C2, NB, acc, rb1, nar, rb2n, rb2, own, cv, qv, patv, offv, patb, ml, sl, st_s, st_r, rs_r,
    qs, qr, qp_s, qp_r,
    az_ss, az_rs, bz_ss, bz_rs, ax_ss, ax_rs, bx_ss, bx_rs, q_ss, q_rs, st_ss, st_rs, rs_ss, rs_rs,
    n1_ss, n1_rs, n2_ss, n2_rs, c_ss, c_rs, qp_ss, qp_rs, loc,
):
    dp = lax.axis_index("dp")
    me = lax.axis_index("cent")
    x, z = me // NZ, me % NZ
    y, core = dp // 2, dp % 2
    sib = (dp + 1 - 2 * core, me)

    def cdev(xx, zz):
        return (dp, xx * NZ + zz)

    loads = [
        pltpu.make_async_copy(src, dst, loc.at[i])
        for i, (src, dst) in enumerate(
            [(p_ref, G.at[z, x]), (q_ref, qv), (c_ref, cv), (pat_ref, patv), (off_ref, offv)]
        )
    ]
    for cp in loads:
        cp.start()

    barrier = pltpu.get_barrier_semaphore()
    for dev in (
        cdev(x, (z + 1) % NZ), cdev(x, (z + NZ - 1) % NZ),
        cdev((x + 1) % NX, z), cdev((x + 2) % NX, z), cdev((x + 3) % NX, z),
    ):
        pl.semaphore_signal(barrier, inc=1, device_id=dev, device_id_type=MESH)
    for o in range(1, DP):
        pl.semaphore_signal(barrier, inc=1, device_id=((dp + o) % DP, me), device_id_type=MESH)
    loads[1].wait()
    qs[...] = jnp.zeros_like(qs)
    qs[0:4, :] = qv[...].astype(F32)
    qr[dp] = qs[...]
    loads[0].wait()
    pl.semaphore_wait(barrier, 5 + DP - 1)

    def q_copy(o, src):
        return rcopy(qs, qr.at[src], q_ss.at[o], q_rs.at[src], ((dp + o) % DP, me))

    def zdev(step):
        return (dp, x * NZ + (z + NZ + step) % NZ)

    def xdev(step):
        return (dp, ((x + NX + step) % NX) * NZ + z)

    STEP = (1, -1)

    def a_z(zs, side, part=None):
        lo, n = (0, D) if part is None else (part * HD, HD)
        ref = G.at[zs, x, pl.ds(0, RA), pl.ds(lo, n)]
        return rcopy(ref, ref, az_ss.at[zs, side], az_rs.at[zs if part != 1 else NZ], zdev(STEP[side]))

    def b_z(zs, side, part):
        ref = G.at[zs, pl.ds(part * (NX // 2), NX // 2), pl.ds(RA, RB)]
        return rcopy(ref, ref, bz_ss.at[zs, side, part], bz_rs.at[zs, part], zdev(STEP[side]))

    def a_x(zs, xs, side):
        ref = G.at[zs, xs, pl.ds(0, RA)]
        return rcopy(ref, ref, ax_ss.at[zs, side], ax_rs.at[zs, side], xdev(STEP[side]))

    def a_x2(zs, xs, side):
        ref = G.at[zs, xs, pl.ds(0, RA), pl.ds(side * HD, HD)]
        return rcopy(ref, ref, ax_ss.at[zs, 2 + side], ax_rs.at[zs, 2 + side], xdev(STEP[side]))

    def b_x(xs, i):
        ref = G.at[z, xs, pl.ds(RA, RB)]
        return rcopy(ref, ref, bx_ss.at[i], bx_rs.at[i], xdev(i))

    def xfrom(side, n=1):
        return (x + NX - n * STEP[side]) % NX

    def zfrom(side, n):
        return (z + NZ - n * STEP[side]) % NZ

    def send_ax(zs):
        for side in range(2):
            a_x(zs, x, side).start()

    def hop_ax(zs):
        for side in range(2):
            a_x(zs, xfrom(side), side).wait_recv()
            a_x2(zs, xfrom(side), side).start()

    def end_ax(zs):
        for side in range(2):
            a_x2(zs, xfrom(side, 2), side).wait_recv()

    def take_a(d):
        for side in range(2):
            zs = zfrom(side, d)
            if d < 4:
                a_z(zs, side).wait_recv()
                a_z(zs, side, None if d < 3 else side).start()
                send_ax(zs)
            else:
                a_z(zs, side, side).wait_recv()
        if d == 4:
            send_ax(zfrom(0, 4))

    def take_b(d):
        for part in range(2):
            for side in range(2):
                zs = zfrom(side, d)
                if d < 4:
                    b_z(zs, side, part).wait_recv()
                    if d < 3 or part == side:
                        b_z(zs, side, part).start()
                elif part == side:
                    b_z(zs, side, part).wait_recv()

    def hop(d):
        for side in range(2 if 0 < d < 4 else 1):
            hop_ax(zfrom(side, d))

    def end(d):
        for side in range(2 if 0 < d < 4 else 1):
            end_ax(zfrom(side, d))

    def gather(compute):
        for side in range(2):
            a_z(z, side).start()
        for i in (2, 1, 3):
            b_x(x, i).start()
        send_ax(z)
        for o in range(1, DP):
            q_copy(o, dp).start()
        take_a(1)
        for i in (1, 3, 2):
            b_x((x + NX - i) % NX, i).wait_recv()
        for part in range(2):
            for side in range(2):
                b_z(z, side, part).start()
        hop(0)
        take_a(2)
        early()
        for d in range(5):
            if d < 4:
                hop(d + 1)
                take_b(d + 1)
            end(d)
            compute(d)
            if d < 2:
                take_a(d + 3)

    def gather_drain():
        for i in range(1, NX):
            b_x(x, i).wait_send()
        for side in range(2):
            for d in range(4):
                zs = zfrom(side, d)
                a_z(zs, side, None if d < 3 else side).wait_send()
                for part in range(2):
                    if d < 3 or part == side:
                        b_z(zs, side, part).wait_send()

        def w(zs, _):
            for side in range(2):
                a_x(zs, x, side).wait_send()
                a_x2(zs, xfrom(side), side).wait_send()
            return 0

        lax.fori_loop(0, NZ, w, 0)

    def q_wait(o, _):
        q_copy(o, (dp + DP - o) % DP).wait_recv()
        return 0

    def early():
        for i in range(2, 5):
            loads[i].wait()
        acc[...] = jnp.zeros_like(acc)
        c0 = cv[...]
        CQ[0:KL, :] = c0.astype(BF16)
        NB[...] = jnp.broadcast_to(jnp.sum(c0 * c0, axis=1, keepdims=True), (KL, 128))
        lane = lax.broadcasted_iota(jnp.int32, (8, BLOCK), 1)
        sub = lax.broadcasted_iota(jnp.int32, (8, BLOCK), 0)
        pick = (lane == me * 4 + sub) & (sub < 4)
        for j in range(DP):
            for i in range(5):
                row = patv[i:i + 1, j * BLOCK:(j + 1) * BLOCK] if i < 4 else offv[j:j + 1, :]
                vals = jnp.where(pick, jnp.broadcast_to(row.astype(F32), (8, BLOCK)), 0.0)
                patb[i, 8 * j:8 * j + 8, :] = jnp.broadcast_to(jnp.sum(vals, axis=1, keepdims=True), (8, BLOCK))
        lax.fori_loop(1, DP, q_wait, 0)
        CQ[KL:KL + QP, :] = qr[...].reshape(QP, D).astype(BF16)

    def column(k):
        d = (k + 1) // 2
        sgn = 1 - 2 * (k % 2)
        return (z + NZ + sgn * d) % NZ

    def st_copy(it, xc, zc, xs, zs):
        return rcopy(
            st_s.at[zc, xc], st_r.at[it, zs, xs], st_ss.at[zc, xc], st_rs.at[it, zs, xs], cdev(xc, zc)
        )

    def logit_part(zc, dots, lo, n, h):
        nb = NB[lo:lo + n, :]
        for xc in range(NX):
            a = xc * BLOCK
            ll = sharpness * (2.0 * dots[0:n, a:a + BLOCK] - nb)
            m = jnp.max(ll, axis=0, keepdims=True)
            e = jnp.exp(ll - m)
            E[zc, lo:lo + n, a:a + BLOCK] = e
            ml[zc, h:h + 1, a:a + BLOCK] = m
            sl[zc, h:h + 1, a:a + BLOCK] = jnp.sum(e, axis=0, keepdims=True)

    def dot_nt(lhs, rhs):
        return lax.dot_general(lhs, rhs, (((1,), (1,)), ((), ())), preferred_element_type=F32)

    def ship(it, zc, mine):
        if mine:
            st_r[it, z, x] = st_s[z, x]
            for i in range(1, NX):
                st_copy(it, (x + i) % NX, z, x, z).start()
        else:
            for xc in range(NX):
                st_copy(it, xc, zc, x, z).start()

    def first_column(zc, mine):
        dots = dot_nt(CQ[...], G[zc].reshape(NX * BLOCK, D))
        logit_part(zc, dots, 0, KL, 0)
        S[zc] = dots[KL:KL + QP, :] * sharpness
        m = ml[zc, 0:1, :]
        s = sl[zc, 0:1, :]
        ml[zc, 1:2, :] = m
        for xc in range(NX):
            st_s[zc, xc, 0:1, :] = m[:, xc * BLOCK:(xc + 1) * BLOCK]
            st_s[zc, xc, 1:2, :] = s[:, xc * BLOCK:(xc + 1) * BLOCK]
        ship(0, zc, mine)

    def softmax_first():
        def compute(d):
            if d == 0:
                first_column(z, True)
            elif d == 4:
                first_column(zfrom(0, 4), False)
            else:
                def side_step(i, _):
                    first_column((z + NZ + (2 * i - 1) * d) % NZ, False)
                    return 0

                lax.fori_loop(0, 2, side_step, 0)

        gather(compute)

    def second_column(zc, h):
        dots = dot_nt(C2[h * RC:(h + 1) * RC, 0:D], G[zc].reshape(NX * BLOCK, D))
        logit_part(zc, dots, h * RC, RC, h)

    def second_ship(zc, mine):
        for xc in range(NX):
            a = xc * BLOCK
            ma, mb = ml[zc, 0:1, a:a + BLOCK], ml[zc, 1:2, a:a + BLOCK]
            m = jnp.maximum(ma, mb)
            st_s[zc, xc, 0:1, :] = m
            st_s[zc, xc, 1:2, :] = (
                sl[zc, 0:1, a:a + BLOCK] * jnp.exp(ma - m) + sl[zc, 1:2, a:a + BLOCK] * jnp.exp(mb - m)
            )
        ship(1, zc, mine)

    def softmax_second():
        for h in range(CH):
            rows_wait(0, h)
            rows = slice(h * RC, (h + 1) * RC)
            NB[rows, :] = jnp.broadcast_to(
                jnp.sum(C2[rows, D:W].astype(F32), axis=1, keepdims=True), (RC, 128)
            )
            if h < CH - 1:
                def part(zc, _):
                    second_column(zc, h)
                    return 0

                lax.fori_loop(0, NZ, part, 0)
            else:
                def last(k, _):
                    zc = column(k)
                    second_column(zc, h)
                    second_ship(zc, False)
                    return 0

                second_column(z, h)
                second_ship(z, True)
                lax.fori_loop(1, NZ, last, 0)

    def rs_copy(it, o, xo, zo):
        peer = (me + o) % CENT
        return rcopy(
            rs_r.at[it, z, x], rs_r.at[it, zo, xo], rs_ss.at[it, o], rs_rs.at[it, zo, xo], (dp, peer)
        )

    def owner_combine(it):
        def w(o, _):
            src = (me + o) % CENT
            st_copy(it, x, z, src // NZ, src % NZ).wait_recv()
            return 0

        lax.fori_loop(1, CENT, w, 0)
        m = st_r[it, :, :, 0:1, :].reshape(CENT, 1, BLOCK)
        s = st_r[it, :, :, 1:2, :].reshape(CENT, 1, BLOCK)
        top = jnp.max(m, axis=0)
        tot = jnp.sum(s * jnp.exp(m - top[None]), axis=0)
        rs_r[it, z, x, 0:1, :] = top
        rs_r[it, z, x, 1:2, :] = 1.0 / tot

        def snd(o, _):
            rs_copy(it, o, x, z).start()
            return 0

        lax.fori_loop(1, CENT, snd, 0)

    def query_post():
        pats = [patb[i] for i in range(4)]
        off = patb[4]
        lane = lax.broadcasted_iota(jnp.int32, (QP, BLOCK), 1)
        lanef = lane.astype(F32)

        def allow_of(b):
            return (pats[0] == b) | (pats[1] == b) | (pats[2] == b) | (pats[3] == b)

        def p1(zc, mx):
            for xc in range(NX):
                b = (dp * CENT + xc * NZ + zc).astype(F32)
                sv = S[zc, :, xc * BLOCK:(xc + 1) * BLOCK]
                mx = jnp.maximum(mx, jnp.where(allow_of(b), sv, NEG))
            return mx

        mx = lax.fori_loop(0, NZ, p1, jnp.full((QP, BLOCK), NEG, F32))
        mrow = jnp.max(mx, axis=1, keepdims=True)
        mb = jnp.broadcast_to(mrow, (QP, BLOCK))

        def p2(zc, carry):
            tot, pos = carry
            for xc in range(NX):
                b = (dp * CENT + xc * NZ + zc).astype(F32)
                sv = S[zc, :, xc * BLOCK:(xc + 1) * BLOCK]
                tot = tot + jnp.where(allow_of(b), jnp.exp(sv - mb), 0.0)
                pos = pos + jnp.where((pats[0] == b) & (lanef == off), sv, 0.0)
            return tot, pos

        zero = jnp.zeros((QP, BLOCK), F32)
        tot, pos = lax.fori_loop(0, NZ, p2, (zero, zero))
        trow = jnp.broadcast_to(jnp.sum(tot, axis=1, keepdims=True), (QP, BLOCK))
        prow = jnp.broadcast_to(jnp.sum(pos, axis=1, keepdims=True), (QP, BLOCK))
        packed = jnp.where(lane == 0, mb, jnp.where(lane == 1, trow, prow))
        qp_s[...] = packed.reshape(DP, 8, BLOCK)
        qp_r[dp] = qp_s[dp]

        def snd(o, _):
            qp_copy(o, (dp + o) % DP, dp).start()
            return 0

        lax.fori_loop(1, DP, snd, 0)

    def qp_copy(o, dst, src):
        return rcopy(qp_s.at[dst], qp_r.at[src], qp_ss.at[o], qp_rs.at[src], (dst, me))

    def query_finish():
        def w(o, _):
            qp_copy(o, (dp + o) % DP, (dp + o) % DP).wait_recv()
            return 0

        lax.fori_loop(1, DP, w, 0)
        m = qp_r[:, :, 0:1]
        t = qp_r[:, :, 1:2]
        p = qp_r[:, :, 2:3]
        top = jnp.max(m, axis=0)
        tot = jnp.sum(t * jnp.exp(m - top[None]), axis=0)
        ps = jnp.sum(p, axis=0)
        loss = jnp.broadcast_to(jnp.log(tot) + top - ps, (8, BLOCK))
        lane = lax.broadcasted_iota(jnp.int32, (8, BLOCK), 1)
        sub = lax.broadcasted_iota(jnp.int32, (8, BLOCK), 0)
        loss_ref[...] = jnp.sum(jnp.where(lane == sub, loss, 0.0), axis=0, keepdims=True)[:, 0:4]

        def ws(o, _):
            qp_copy(o, (dp + o) % DP, dp).wait_send()
            return 0

        lax.fori_loop(1, DP, ws, 0)

    def stats_wait(it):
        def w(o, _):
            src = (me + o) % CENT
            rs_copy(it, o, src // NZ, src % NZ).wait_recv()
            return 0

        lax.fori_loop(1, CENT, w, 0)

    def stats_drain(it):
        def ws(o, _):
            dst = (me + o) % CENT
            st_copy(it, dst // NZ, dst % NZ, x, z).wait_send()
            rs_copy(it, o, x, z).wait_send()
            return 0

        lax.fori_loop(1, CENT, ws, 0)

    def numer(it, h, lo, hi):
        rows = slice(h * RC, (h + 1) * RC)

        def col(zc, _):
            cnt = acc[it, rows, D:W]
            parts = []
            for xc in range(NX):
                a = xc * BLOCK
                g = jnp.exp(ml[zc, h:h + 1, a:a + BLOCK] - rs_r[it, zc, xc, 0:1, :]) * rs_r[it, zc, xc, 1:2, :]
                r = E[zc, rows, a:a + BLOCK] * g
                cnt = cnt + r
                parts.append(r.astype(BF16))
            acc[it, rows, D:W] = cnt
            r_all = jnp.concatenate(parts, axis=1)
            acc[it, rows, 0:D] += jnp.dot(r_all, G[zc].reshape(NX * BLOCK, D), preferred_element_type=F32)
            return 0

        lax.fori_loop(lo, hi, col, 0)

    mine_at = [pl.multiple_of(h * RC + core * RH, RH) for h in range(CH)]
    theirs_at = [pl.multiple_of(h * RC + RH - core * RH, RH) for h in range(CH)]

    def pair_copy(it, h):
        return rcopy(acc.at[it, pl.ds(theirs_at[h], RH)], rb1.at[it, h], n1_ss.at[it, h], n1_rs.at[it, h], sib)

    def quarter(h, yy):
        return pl.ds(pl.multiple_of(h * RC + core * RH + yy * RQ, RQ), RQ)

    def y_copy(it, h, i):
        yp = (y + i) % NY
        sem = (n2_ss.at[it, h, i], n2_rs.at[it, h, i])
        if NARROW[it]:
            src = nar.at[it, h, pl.ds(pl.multiple_of(yp * RQ, RQ), RQ)]
            return rcopy(src, rb2n.at[it, h, i], *sem, (yp * 2 + core, me))
        return rcopy(acc.at[it, quarter(h, yp)], rb2.at[it, h, i], *sem, (yp * 2 + core, me))

    def pair_sum(it, h):
        pair_copy(it, h).wait_recv()
        tot = acc[it, pl.ds(mine_at[h], RH), :] + rb1[it, h]
        acc[it, pl.ds(mine_at[h], RH), :] = tot
        if NARROW[it]:
            nar[it, h, :, 0:D] = tot[:, 0:D].astype(BF16)
            nar[it, h, :, D:W] = three(jnp.sum(tot[:, D:W], axis=1, keepdims=True), RH)
        for i in (2, 1, 3):
            y_copy(it, h, i).start()

    def update(it, h):
        tot = acc[it, quarter(h, y), :]
        for i in (1, 3, 2):
            y_copy(it, h, i).wait_recv()
            tot = tot + (rb2n[it, h, i].astype(F32) if NARROW[it] else rb2[it, h, i])
        counts = jnp.sum(tot[:, D:W], axis=1, keepdims=True)
        cold = cv[quarter(h, y), :] if it == 0 else own[h]
        return (tot[:, 0:D] + cold) / (counts + 1.0)

    def row_copy(k, h, i):
        arr = C2 if k == 0 else out_ref
        ref = arr.at[quarter(h, y)]
        return rcopy(ref, ref, c_ss.at[k, h, i], c_rs.at[k, h, i], (((y + i) % NY) * 2 + core, me))

    def half_copy(k, h):
        arr = C2 if k == 0 else out_ref
        ref = arr.at[pl.ds(mine_at[h], RH)]
        return rcopy(ref, ref, c_ss.at[k, h, 0], c_rs.at[k, h, 0], sib)

    def rows_send(k, h):
        for i in (2, 1, 3):
            row_copy(k, h, i).start()

    def rows_pass(k, h):
        for i in (1, 3, 2):
            row_copy(k, h, i).wait_recv()
        half_copy(k, h).start()

    def rows_wait(k, h):
        half_copy(k, h).wait_recv()

    def reduce_drain(it):
        for h in range(CH):
            pair_copy(it, h).wait_send()
            for i in range(1, NY):
                y_copy(it, h, i).wait_send()
                row_copy(it, h, i).wait_send()
            half_copy(it, h).wait_send()

    def finish():
        if STOP >= 0:
            gather_drain()

        def wsq(o, _):
            q_copy(o, dp).wait_send()
            return 0

        lax.fori_loop(1, DP, wsq, 0)
        if STOP < 90:
            out_ref[...] = jnp.zeros_like(out_ref)
            loss_ref[...] = jnp.zeros_like(loss_ref)

    def mid(it):
        numer(it, 0, 0, NZ)
        pair_copy(it, 0).start()
        numer(it, 1, 0, NZ // 2)
        pair_sum(it, 0)
        numer(it, 1, NZ // 2, NZ)
        pair_copy(it, 1).start()
        pair_sum(it, 1)

    if STOP == -2:
        for o in range(1, DP):
            q_copy(o, dp).start()
        lax.fori_loop(1, DP, q_wait, 0)
        for i in range(2, 5):
            loads[i].wait()
        return finish()
    if STOP == -1:
        for o in range(1, DP):
            q_copy(o, dp).start()
        early()
        return finish()
    if STOP == 0:
        gather(lambda d: None)
        return finish()
    softmax_first()
    owner_combine(0)
    if STOP == 1:
        stats_wait(0)
        stats_drain(0)
        return finish()
    query_post()
    stats_wait(0)
    if STOP == 2:
        stats_drain(0)
        query_finish()
        return finish()
    mid(0)
    for h in range(CH):
        newc = update(0, h)
        own[h] = newc
        C2[quarter(h, y), 0:D] = newc.astype(BF16)
        C2[quarter(h, y), D:W] = three(jnp.sum(newc * newc, axis=1, keepdims=True), RQ)
        rows_send(0, h)
    stats_drain(0)
    for h in range(CH):
        rows_pass(0, h)
    if STOP == 5:
        for h in range(CH):
            rows_wait(0, h)
        reduce_drain(0)
        query_finish()
        return finish()

    softmax_second()
    owner_combine(1)
    query_finish()
    stats_wait(1)
    if STOP == 6:
        stats_drain(1)
        reduce_drain(0)
        return finish()
    mid(1)
    for h in range(CH):
        out_ref[quarter(h, y), :] = update(1, h).astype(BF16)
        rows_send(1, h)
    stats_drain(1)
    reduce_drain(0)
    for h in range(CH):
        rows_pass(1, h)
    for h in range(CH):
        rows_wait(1, h)
    reduce_drain(1)
    finish()


def on_device(passages, queries, init_centroids, pattern, positive_offset):
    vm = pl.BlockSpec(memory_space=pltpu.VMEM)
    anywhere = pl.BlockSpec(memory_space=pl.ANY)
    dma = pltpu.SemaphoreType.DMA
    centroids, loss = pl.pallas_call(
        kernel,
        out_shape=(jax.ShapeDtypeStruct((KL, D), BF16), jax.ShapeDtypeStruct((1, 4), F32)),
        in_specs=[anywhere] * 5,
        out_specs=(vm, vm),
        scratch_shapes=[
            pltpu.VMEM((NZ, NX, BLOCK, D), BF16),
            pltpu.VMEM((NZ, KL, NX * BLOCK), F32),
            pltpu.VMEM((NZ, QP, NX * BLOCK), F32),
            pltpu.VMEM((KL + QP, D), BF16),
            pltpu.VMEM((KL, W), BF16),
            pltpu.VMEM((KL, 128), F32),
            pltpu.VMEM((2, KL, W), F32),
            pltpu.VMEM((2, CH, RH, W), F32),
            pltpu.VMEM((2, CH, RH, W), BF16),
            pltpu.VMEM((2, CH, NY, RQ, W), BF16),
            pltpu.VMEM((2, CH, NY, RQ, W), F32),
            pltpu.VMEM((CH, RQ, D), F32),
            pltpu.VMEM((KL, D), F32),
            pltpu.VMEM((4, D), BF16),
            pltpu.VMEM((4, 1024), jnp.int32),
            pltpu.VMEM((DP, 128), jnp.int32),
            pltpu.VMEM((5, QP, 128), F32),
            pltpu.VMEM((NZ, CH, NX * BLOCK), F32),
            pltpu.VMEM((NZ, CH, NX * BLOCK), F32),
            pltpu.VMEM((NZ, NX, 2, 128), F32),
            pltpu.VMEM((2, NZ, NX, 2, 128), F32),
            pltpu.VMEM((2, NZ, NX, 2, 128), F32),
            pltpu.VMEM((8, D), F32),
            pltpu.VMEM((DP, 8, D), F32),
            pltpu.VMEM((DP, 8, 128), F32),
            pltpu.VMEM((DP, 8, 128), F32),
            dma((NZ, 2)), dma((NZ + 1,)), dma((NZ, 2, 2)), dma((NZ, 2)),
            dma((NZ, 4)), dma((NZ, 4)), dma((4,)), dma((4,)),
            dma((DP,)), dma((DP,)),
            dma((NZ, NX)), dma((2, NZ, NX)),
            dma((2, CENT)), dma((2, NZ, NX)),
            dma((2, CH)), dma((2, CH)),
            dma((2, CH, NY)), dma((2, CH, NY)),
            dma((2, CH, NY)), dma((2, CH, NY)),
            dma((DP,)), dma((DP,)),
            dma((5,)),
        ],
        compiler_params=pltpu.CompilerParams(
            collective_id=0, has_side_effects=True, vmem_limit_bytes=56 * 1024 * 1024
        ),
    )(passages, queries, init_centroids, pattern.T, positive_offset.reshape(DP, 128))
    return centroids.astype(F32), loss.reshape(4)


def solution(mesh):
    placed = (P(("dp", "cent"), None), P(("dp", "cent"), None), P("cent", None), P(), P())
    return jax.shard_map(
        on_device,
        mesh=mesh,
        in_specs=placed,
        out_specs=(P("cent", None), P(("dp", "cent"))),
        check_vma=False,
    )
```

```python
import jax
import jax.numpy as jnp
from jax import lax
from jax.experimental import pallas as pl
from jax.experimental.pallas import tpu as pltpu
from jax.sharding import PartitionSpec as P

MESH = pl.DeviceIdType.MESH
BLOCK = 128
D = 768
HD = 384
NX, NZ, NY = 4, 8, 4
CENT = NX * NZ
DP = 2 * NY
KL = 256
QP = 64
W = D + 128
CH = 2
RC = KL // CH
RH = RC // 2
RQ = RH // NY
sharpness = 0.05
NEG = -1e30
STOP = 99
RA = 80
RB = 128 - RA
NARROW = (True, False)
F32 = jnp.float32
BF16 = jnp.bfloat16


def rcopy(src, dst, ss, rs, dev):
    return pltpu.make_async_remote_copy(
        src_ref=src, dst_ref=dst, send_sem=ss, recv_sem=rs, device_id=dev, device_id_type=MESH
    )


def three(v, rows):
    lane = lax.broadcasted_iota(jnp.int32, (rows, 128), 1)
    v = jnp.broadcast_to(v, (rows, 128))
    hi = v.astype(BF16).astype(F32)
    mid = (v - hi).astype(BF16).astype(F32)
    lo = v - hi - mid
    return jnp.where(lane == 0, hi, jnp.where(lane == 1, mid, jnp.where(lane == 2, lo, 0.0))).astype(BF16)


def kernel(
    p_ref, q_ref, c_ref, pat_ref, off_ref, out_ref, loss_ref,
    G, E, S, CQ, C2, NB, acc, rb1, nar, rb2n, rb2, own, cv, qv, patv, offv, patb, st_s, st_r, rs_r,
    qs, qr, qp_s, qp_r,
    az_ss, az_rs, bz_ss, bz_rs, ax_ss, ax_rs, bx_ss, bx_rs, q_ss, q_rs, st_ss, st_rs, rs_ss, rs_rs,
    n1_ss, n1_rs, n2_ss, n2_rs, c_ss, c_rs, qp_ss, qp_rs, loc,
):
    dp = lax.axis_index("dp")
    me = lax.axis_index("cent")
    x, z = me // NZ, me % NZ
    y, core = dp // 2, dp % 2
    sib = (dp + 1 - 2 * core, me)

    def cdev(xx, zz):
        return (dp, xx * NZ + zz)

    loads = [
        pltpu.make_async_copy(src, dst, loc.at[i])
        for i, (src, dst) in enumerate(
            [(p_ref, G.at[z, x]), (q_ref, qv), (c_ref, cv), (pat_ref, patv), (off_ref, offv)]
        )
    ]
    for cp in loads:
        cp.start()

    barrier = pltpu.get_barrier_semaphore()
    for dev in (
        cdev(x, (z + 1) % NZ), cdev(x, (z + NZ - 1) % NZ),
        cdev((x + 1) % NX, z), cdev((x + 2) % NX, z), cdev((x + 3) % NX, z),
    ):
        pl.semaphore_signal(barrier, inc=1, device_id=dev, device_id_type=MESH)
    for o in range(1, DP):
        pl.semaphore_signal(barrier, inc=1, device_id=((dp + o) % DP, me), device_id_type=MESH)
    loads[1].wait()
    qs[...] = jnp.zeros_like(qs)
    qs[0:4, :] = qv[...].astype(F32)
    qr[dp] = qs[...]
    loads[0].wait()
    pl.semaphore_wait(barrier, 5 + DP - 1)

    def q_copy(o, src):
        return rcopy(qs, qr.at[src], q_ss.at[o], q_rs.at[src], ((dp + o) % DP, me))

    def zdev(step):
        return (dp, x * NZ + (z + NZ + step) % NZ)

    def xdev(step):
        return (dp, ((x + NX + step) % NX) * NZ + z)

    STEP = (1, -1)

    def a_z(zs, side, part=None):
        lo, n = (0, D) if part is None else (part * HD, HD)
        ref = G.at[zs, x, pl.ds(0, RA), pl.ds(lo, n)]
        return rcopy(ref, ref, az_ss.at[zs, side], az_rs.at[zs if part != 1 else NZ], zdev(STEP[side]))

    def b_z(zs, side, part):
        ref = G.at[zs, pl.ds(part * (NX // 2), NX // 2), pl.ds(RA, RB)]
        return rcopy(ref, ref, bz_ss.at[zs, side, part], bz_rs.at[zs, part], zdev(STEP[side]))

    def a_x(zs, xs, side):
        ref = G.at[zs, xs, pl.ds(0, RA)]
        return rcopy(ref, ref, ax_ss.at[zs, side], ax_rs.at[zs, side], xdev(STEP[side]))

    def a_x2(zs, xs, side):
        ref = G.at[zs, xs, pl.ds(0, RA), pl.ds(side * HD, HD)]
        return rcopy(ref, ref, ax_ss.at[zs, 2 + side], ax_rs.at[zs, 2 + side], xdev(STEP[side]))

    def b_x(xs, i):
        ref = G.at[z, xs, pl.ds(RA, RB)]
        return rcopy(ref, ref, bx_ss.at[i], bx_rs.at[i], xdev(i))

    def xfrom(side, n=1):
        return (x + NX - n * STEP[side]) % NX

    def zfrom(side, n):
        return (z + NZ - n * STEP[side]) % NZ

    def send_ax(zs):
        for side in range(2):
            a_x(zs, x, side).start()

    def hop_ax(zs):
        for side in range(2):
            a_x(zs, xfrom(side), side).wait_recv()
            a_x2(zs, xfrom(side), side).start()

    def end_ax(zs):
        for side in range(2):
            a_x2(zs, xfrom(side, 2), side).wait_recv()

    def take_a(d):
        for side in range(2):
            zs = zfrom(side, d)
            if d < 4:
                a_z(zs, side).wait_recv()
                a_z(zs, side, None if d < 3 else side).start()
                send_ax(zs)
            else:
                a_z(zs, side, side).wait_recv()
        if d == 4:
            send_ax(zfrom(0, 4))

    def take_b(d, part):
        for side in range(2):
            zs = zfrom(side, d)
            if d < 4:
                b_z(zs, side, part).wait_recv()
                if d < 3 or part == side:
                    b_z(zs, side, part).start()
            elif part == side:
                b_z(zs, side, part).wait_recv()

    def hop(d):
        for side in range(2 if 0 < d < 4 else 1):
            hop_ax(zfrom(side, d))

    def end(d):
        for side in range(2 if 0 < d < 4 else 1):
            end_ax(zfrom(side, d))

    def gather(compute):
        for side in range(2):
            a_z(z, side).start()
        for i in (2, 1, 3):
            b_x(x, i).start()
        send_ax(z)
        for o in range(1, DP):
            q_copy(o, dp).start()
        take_a(1)
        for i in (1, 3, 2):
            b_x((x + NX - i) % NX, i).wait_recv()
        for part in range(2):
            for side in range(2):
                b_z(z, side, part).start()
        take_a(2)
        hop(0)
        early()
        take_b(1, 0)
        take_b(1, 1)
        hop(1)
        hop(2)
        take_a(3)
        take_b(2, 0)
        take_b(2, 1)
        take_a(4)
        take_b(3, 0)
        end(1)
        hop(3)
        end(0)
        end(2)
        compute(2)
        take_b(3, 1)
        hop(4)
        compute(0)
        compute(1)
        end(3)
        compute(3)
        take_b(4, 0)
        take_b(4, 1)
        end(4)
        compute(4)

    def gather_drain():
        for i in range(1, NX):
            b_x(x, i).wait_send()
        for side in range(2):
            for d in range(4):
                zs = zfrom(side, d)
                a_z(zs, side, None if d < 3 else side).wait_send()
                for part in range(2):
                    if d < 3 or part == side:
                        b_z(zs, side, part).wait_send()

        def w(zs, _):
            for side in range(2):
                a_x(zs, x, side).wait_send()
                a_x2(zs, xfrom(side), side).wait_send()
            return 0

        lax.fori_loop(0, NZ, w, 0)

    def q_wait(o, _):
        q_copy(o, (dp + DP - o) % DP).wait_recv()
        return 0

    def early():
        for i in range(2, 5):
            loads[i].wait()
        c0 = cv[...]
        CQ[0:KL, :] = c0.astype(BF16)
        NB[...] = jnp.broadcast_to(jnp.sum(c0 * c0, axis=1, keepdims=True), (KL, 128))
        lane = lax.broadcasted_iota(jnp.int32, (8, BLOCK), 1)
        sub = lax.broadcasted_iota(jnp.int32, (8, BLOCK), 0)
        pick = (lane == me * 4 + sub) & (sub < 4)
        for j in range(DP):
            for i in range(5):
                row = patv[i:i + 1, j * BLOCK:(j + 1) * BLOCK] if i < 4 else offv[j:j + 1, :]
                vals = jnp.where(pick, jnp.broadcast_to(row.astype(F32), (8, BLOCK)), 0.0)
                patb[i, 8 * j:8 * j + 8, :] = jnp.broadcast_to(jnp.sum(vals, axis=1, keepdims=True), (8, BLOCK))
        lax.fori_loop(1, DP, q_wait, 0)
        CQ[KL:KL + QP, :] = qr[...].reshape(QP, D).astype(BF16)

    def column(k):
        d = (k + 1) // 2
        sgn = 1 - 2 * (k % 2)
        return (z + NZ + sgn * d) % NZ

    def st_copy(it, xc, zc, xs, zs):
        return rcopy(
            st_s.at[zc, xc], st_r.at[it, zs, xs], st_ss.at[zc, xc], st_rs.at[it, zs, xs], cdev(xc, zc)
        )

    def dot_nt(lhs, rhs):
        return lax.dot_general(lhs, rhs, (((1,), (1,)), ((), ())), preferred_element_type=F32)

    def ship(it, zc, mine):
        if mine:
            st_r[it, z, x] = st_s[z, x]
            for i in range(1, NX):
                st_copy(it, (x + i) % NX, z, x, z).start()
        else:
            for xc in range(NX):
                st_copy(it, xc, zc, x, z).start()

    def columns(it, zcs):
        for zc in zcs:
            lhs = CQ[...] if it == 0 else C2[:, 0:D]
            dots = dot_nt(lhs, G[zc].reshape(NX * BLOCK, D))
            nb = NB[...]
            for xc in range(NX):
                a = xc * BLOCK
                ll = sharpness * (2.0 * dots[0:KL, a:a + BLOCK] - nb)
                m = jnp.max(ll, axis=0, keepdims=True)
                e = jnp.exp(ll - m)
                E[zc, :, a:a + BLOCK] = e
                st_s[zc, xc, 0:1, :] = m
                st_s[zc, xc, 1:2, :] = jnp.sum(e, axis=0, keepdims=True)
            if it == 0:
                S[zc] = dots[KL:KL + QP, :] * sharpness

    def softmax_first():
        def compute(d):
            zcs = [zfrom(side, d) for side in range(2 if 0 < d < 4 else 1)]
            columns(0, zcs)
            for zc in zcs:
                ship(0, zc, d == 0)

        gather(compute)

    def softmax_second():
        for h in range(CH):
            rows_wait(0, h)
        NB[...] = jnp.broadcast_to(jnp.sum(C2[:, D:W].astype(F32), axis=1, keepdims=True), (KL, 128))
        for grp in ((7, 6, 5, 4), (3, 2, 1, 0)):
            columns(1, [column(k) for k in grp])
            for k in grp:
                ship(1, column(k), k == 0)

    def rs_copy(it, o, xo, zo):
        dev = cdev((x + o // NZ) % NX, (z + o % NZ) % NZ)
        return rcopy(rs_r.at[it, z, x], rs_r.at[it, zo, xo], rs_ss.at[it, o], rs_rs.at[it, zo, xo], dev)

    def owner_combine(it):
        def w(o, _):
            src = (me + o) % CENT
            st_copy(it, x, z, src // NZ, src % NZ).wait_recv()
            return 0

        lax.fori_loop(1, CENT, w, 0)
        m = st_r[it, :, :, 0:1, :].reshape(CENT, 1, BLOCK)
        s = st_r[it, :, :, 1:2, :].reshape(CENT, 1, BLOCK)
        top = jnp.max(m, axis=0)
        tot = jnp.sum(s * jnp.exp(m - top[None]), axis=0)
        rs_r[it, z, x, 0:1, :] = top
        rs_r[it, z, x, 1:2, :] = 1.0 / tot

        for dz in (4, 3, 5, 2, 6, 1, 7, 0):
            for dx in (2, 1, 3, 0):
                if dz or dx:
                    rs_copy(it, dx * NZ + dz, x, z).start()

    def query_post():
        pats = [patb[i] for i in range(4)]
        off = patb[4]
        lane = lax.broadcasted_iota(jnp.int32, (QP, BLOCK), 1)
        lanef = lane.astype(F32)

        def allow_of(b):
            return (pats[0] == b) | (pats[1] == b) | (pats[2] == b) | (pats[3] == b)

        def p1(zc, mx):
            for xc in range(NX):
                b = (dp * CENT + xc * NZ + zc).astype(F32)
                sv = S[zc, :, xc * BLOCK:(xc + 1) * BLOCK]
                mx = jnp.maximum(mx, jnp.where(allow_of(b), sv, NEG))
            return mx

        mx = lax.fori_loop(0, NZ, p1, jnp.full((QP, BLOCK), NEG, F32))
        mrow = jnp.max(mx, axis=1, keepdims=True)
        mb = jnp.broadcast_to(mrow, (QP, BLOCK))

        def p2(zc, carry):
            tot, pos = carry
            for xc in range(NX):
                b = (dp * CENT + xc * NZ + zc).astype(F32)
                sv = S[zc, :, xc * BLOCK:(xc + 1) * BLOCK]
                tot = tot + jnp.where(allow_of(b), jnp.exp(sv - mb), 0.0)
                pos = pos + jnp.where((pats[0] == b) & (lanef == off), sv, 0.0)
            return tot, pos

        zero = jnp.zeros((QP, BLOCK), F32)
        tot, pos = lax.fori_loop(0, NZ, p2, (zero, zero))
        trow = jnp.broadcast_to(jnp.sum(tot, axis=1, keepdims=True), (QP, BLOCK))
        prow = jnp.broadcast_to(jnp.sum(pos, axis=1, keepdims=True), (QP, BLOCK))
        packed = jnp.where(lane == 0, mb, jnp.where(lane == 1, trow, prow))
        qp_s[...] = packed.reshape(DP, 8, BLOCK)
        qp_r[dp] = qp_s[dp]

        def snd(o, _):
            qp_copy(o, (dp + o) % DP, dp).start()
            return 0

        lax.fori_loop(1, DP, snd, 0)

    def qp_copy(o, dst, src):
        return rcopy(qp_s.at[dst], qp_r.at[src], qp_ss.at[o], qp_rs.at[src], (dst, me))

    def query_finish():
        def w(o, _):
            qp_copy(o, (dp + o) % DP, (dp + o) % DP).wait_recv()
            return 0

        lax.fori_loop(1, DP, w, 0)
        m = qp_r[:, :, 0:1]
        t = qp_r[:, :, 1:2]
        p = qp_r[:, :, 2:3]
        top = jnp.max(m, axis=0)
        tot = jnp.sum(t * jnp.exp(m - top[None]), axis=0)
        ps = jnp.sum(p, axis=0)
        loss = jnp.broadcast_to(jnp.log(tot) + top - ps, (8, BLOCK))
        lane = lax.broadcasted_iota(jnp.int32, (8, BLOCK), 1)
        sub = lax.broadcasted_iota(jnp.int32, (8, BLOCK), 0)
        loss_ref[...] = jnp.sum(jnp.where(lane == sub, loss, 0.0), axis=0, keepdims=True)[:, 0:4]

        def ws(o, _):
            qp_copy(o, (dp + o) % DP, dp).wait_send()
            return 0

        lax.fori_loop(1, DP, ws, 0)

    def stats_wait(it):
        def w(o, _):
            src = (me + o) % CENT
            rs_copy(it, o, src // NZ, src % NZ).wait_recv()
            return 0

        lax.fori_loop(1, CENT, w, 0)

    def stats_drain(it):
        def ws(o, _):
            dst = (me + o) % CENT
            st_copy(it, dst // NZ, dst % NZ, x, z).wait_send()
            rs_copy(it, o, x, z).wait_send()
            return 0

        lax.fori_loop(1, CENT, ws, 0)

    def numer(it, h):
        rows = slice(h * RC, (h + 1) * RC)
        cnt = jnp.zeros((RC, BLOCK), F32)
        tot = jnp.zeros((RC, D), F32)
        for zc in range(NZ):
            parts = []
            for xc in range(NX):
                a = xc * BLOCK
                g = jnp.exp(st_s[zc, xc, 0:1, :] - rs_r[it, zc, xc, 0:1, :]) * rs_r[it, zc, xc, 1:2, :]
                r = E[zc, rows, a:a + BLOCK] * g
                cnt = cnt + r
                parts.append(r.astype(BF16))
            tot = tot + jnp.dot(
                jnp.concatenate(parts, axis=1), G[zc].reshape(NX * BLOCK, D), preferred_element_type=F32
            )
        acc[it, rows, 0:D] = tot
        acc[it, rows, D:W] = cnt

    mine_at = [pl.multiple_of(h * RC + core * RH, RH) for h in range(CH)]
    theirs_at = [pl.multiple_of(h * RC + RH - core * RH, RH) for h in range(CH)]

    def pair_copy(it, h):
        return rcopy(acc.at[it, pl.ds(theirs_at[h], RH)], rb1.at[it, h], n1_ss.at[it, h], n1_rs.at[it, h], sib)

    def quarter(h, yy):
        return pl.ds(pl.multiple_of(h * RC + core * RH + yy * RQ, RQ), RQ)

    def y_copy(it, h, i):
        yp = (y + i) % NY
        sem = (n2_ss.at[it, h, i], n2_rs.at[it, h, i])
        if NARROW[it]:
            src = nar.at[it, h, pl.ds(pl.multiple_of(yp * RQ, RQ), RQ)]
            return rcopy(src, rb2n.at[it, h, i], *sem, (yp * 2 + core, me))
        return rcopy(acc.at[it, quarter(h, yp)], rb2.at[it, h, i], *sem, (yp * 2 + core, me))

    def pair_sum(it, h):
        pair_copy(it, h).wait_recv()
        tot = acc[it, pl.ds(mine_at[h], RH), :] + rb1[it, h]
        acc[it, pl.ds(mine_at[h], RH), :] = tot
        if NARROW[it]:
            nar[it, h, :, 0:D] = tot[:, 0:D].astype(BF16)
            nar[it, h, :, D:W] = three(jnp.sum(tot[:, D:W], axis=1, keepdims=True), RH)
        for i in (2, 1, 3):
            y_copy(it, h, i).start()

    def update(it, h):
        tot = acc[it, quarter(h, y), :]
        for i in (1, 3, 2):
            y_copy(it, h, i).wait_recv()
            tot = tot + (rb2n[it, h, i].astype(F32) if NARROW[it] else rb2[it, h, i])
        counts = jnp.sum(tot[:, D:W], axis=1, keepdims=True)
        cold = cv[quarter(h, y), :] if it == 0 else own[h]
        return (tot[:, 0:D] + cold) / (counts + 1.0)

    def row_copy(k, h, i):
        arr = C2 if k == 0 else out_ref
        ref = arr.at[quarter(h, y)]
        return rcopy(ref, ref, c_ss.at[k, h, i], c_rs.at[k, h, i], (((y + i) % NY) * 2 + core, me))

    def half_copy(k, h):
        arr = C2 if k == 0 else out_ref
        ref = arr.at[pl.ds(mine_at[h], RH)]
        return rcopy(ref, ref, c_ss.at[k, h, 0], c_rs.at[k, h, 0], sib)

    def rows_send(k, h):
        for i in (2, 1, 3):
            row_copy(k, h, i).start()

    def rows_pass(k, h):
        for i in (1, 3, 2):
            row_copy(k, h, i).wait_recv()
        half_copy(k, h).start()

    def rows_wait(k, h):
        half_copy(k, h).wait_recv()

    def reduce_drain(it):
        for h in range(CH):
            pair_copy(it, h).wait_send()
            for i in range(1, NY):
                y_copy(it, h, i).wait_send()
                row_copy(it, h, i).wait_send()
            half_copy(it, h).wait_send()

    def finish():
        if STOP < 1:
            early_drain()
        if STOP < 90:
            out_ref[...] = jnp.zeros_like(out_ref)
            loss_ref[...] = jnp.zeros_like(loss_ref)

    def early_drain():
        if STOP >= 0:
            gather_drain()

        def wsq(o, _):
            q_copy(o, dp).wait_send()
            return 0

        lax.fori_loop(1, DP, wsq, 0)

    def mid(it):
        for h in range(CH):
            numer(it, h)
            pair_copy(it, h).start()
        for h in range(CH):
            pair_sum(it, h)

    if STOP == -2:
        for o in range(1, DP):
            q_copy(o, dp).start()
        lax.fori_loop(1, DP, q_wait, 0)
        for i in range(2, 5):
            loads[i].wait()
        return finish()
    if STOP == -1:
        for o in range(1, DP):
            q_copy(o, dp).start()
        early()
        return finish()
    if STOP == 0:
        gather(lambda d: None)
        return finish()
    softmax_first()
    owner_combine(0)
    early_drain()
    if STOP == 1:
        stats_wait(0)
        stats_drain(0)
        return finish()
    query_post()
    stats_wait(0)
    if STOP == 2:
        stats_drain(0)
        query_finish()
        return finish()
    mid(0)
    for h in range(CH):
        newc = update(0, h)
        own[h] = newc
        C2[quarter(h, y), 0:D] = newc.astype(BF16)
        C2[quarter(h, y), D:W] = three(jnp.sum(newc * newc, axis=1, keepdims=True), RQ)
        rows_send(0, h)
    stats_drain(0)
    for h in range(CH):
        rows_pass(0, h)
    if STOP == 5:
        for h in range(CH):
            rows_wait(0, h)
        reduce_drain(0)
        query_finish()
        return finish()

    softmax_second()
    owner_combine(1)
    query_finish()
    stats_wait(1)
    if STOP == 6:
        stats_drain(1)
        reduce_drain(0)
        return finish()
    mid(1)
    for h in range(CH):
        out_ref[quarter(h, y), :] = update(1, h).astype(BF16)
        rows_send(1, h)
    stats_drain(1)
    reduce_drain(0)
    for h in range(CH):
        rows_pass(1, h)
    for h in range(CH):
        rows_wait(1, h)
    reduce_drain(1)
    finish()


def on_device(passages, queries, init_centroids, pattern, positive_offset):
    vm = pl.BlockSpec(memory_space=pltpu.VMEM)
    anywhere = pl.BlockSpec(memory_space=pl.ANY)
    dma = pltpu.SemaphoreType.DMA
    centroids, loss = pl.pallas_call(
        kernel,
        out_shape=(jax.ShapeDtypeStruct((KL, D), BF16), jax.ShapeDtypeStruct((1, 4), F32)),
        in_specs=[anywhere] * 5,
        out_specs=(vm, vm),
        scratch_shapes=[
            pltpu.VMEM((NZ, NX, BLOCK, D), BF16),
            pltpu.VMEM((NZ, KL, NX * BLOCK), F32),
            pltpu.VMEM((NZ, QP, NX * BLOCK), F32),
            pltpu.VMEM((KL + QP, D), BF16),
            pltpu.VMEM((KL, W), BF16),
            pltpu.VMEM((KL, 128), F32),
            pltpu.VMEM((2, KL, W), F32),
            pltpu.VMEM((2, CH, RH, W), F32),
            pltpu.VMEM((2, CH, RH, W), BF16),
            pltpu.VMEM((2, CH, NY, RQ, W), BF16),
            pltpu.VMEM((2, CH, NY, RQ, W), F32),
            pltpu.VMEM((CH, RQ, D), F32),
            pltpu.VMEM((KL, D), F32),
            pltpu.VMEM((4, D), BF16),
            pltpu.VMEM((4, 1024), jnp.int32),
            pltpu.VMEM((DP, 128), jnp.int32),
            pltpu.VMEM((5, QP, 128), F32),
            pltpu.VMEM((NZ, NX, 2, 128), F32),
            pltpu.VMEM((2, NZ, NX, 2, 128), F32),
            pltpu.VMEM((2, NZ, NX, 2, 128), F32),
            pltpu.VMEM((8, D), F32),
            pltpu.VMEM((DP, 8, D), F32),
            pltpu.VMEM((DP, 8, 128), F32),
            pltpu.VMEM((DP, 8, 128), F32),
            dma((NZ, 2)), dma((NZ + 1,)), dma((NZ, 2, 2)), dma((NZ, 2)),
            dma((NZ, 4)), dma((NZ, 4)), dma((4,)), dma((4,)),
            dma((DP,)), dma((DP,)),
            dma((NZ, NX)), dma((2, NZ, NX)),
            dma((2, CENT)), dma((2, NZ, NX)),
            dma((2, CH)), dma((2, CH)),
            dma((2, CH, NY)), dma((2, CH, NY)),
            dma((2, CH, NY)), dma((2, CH, NY)),
            dma((DP,)), dma((DP,)),
            dma((5,)),
        ],
        compiler_params=pltpu.CompilerParams(
            collective_id=0, has_side_effects=True, vmem_limit_bytes=56 * 1024 * 1024
        ),
    )(passages, queries, init_centroids, pattern.T, positive_offset.reshape(DP, 128))
    return centroids.astype(F32), loss.reshape(4)


def solution(mesh):
    placed = (P(("dp", "cent"), None), P(("dp", "cent"), None), P("cent", None), P(), P())
    return jax.shard_map(
        on_device,
        mesh=mesh,
        in_specs=placed,
        out_specs=(P("cent", None), P(("dp", "cent"))),
        check_vma=False,
    )
```

```python
import jax
import jax.numpy as jnp
from jax import lax
from jax.experimental import pallas as pl
from jax.experimental.pallas import tpu as pltpu
from jax.sharding import PartitionSpec as P

MESH = pl.DeviceIdType.MESH
BLOCK = 128
D = 768
HD = 384
NX, NZ, NY = 4, 8, 4
CENT = NX * NZ
DP = 2 * NY
KL = 256
QP = 64
W = D + 128
CH = 2
RC = KL // CH
RH = RC // 2
RQ = RH // NY
sharpness = 0.05
NEG = -1e30
STOP = 99
RA = 80
RB = 128 - RA
NARROW = (True, False)
FAR, NEAR = (0, 1, 2, 3), (4, 5, 6, 7)
F32 = jnp.float32
BF16 = jnp.bfloat16


def rcopy(src, dst, ss, rs, dev):
    return pltpu.make_async_remote_copy(
        src_ref=src, dst_ref=dst, send_sem=ss, recv_sem=rs, device_id=dev, device_id_type=MESH
    )


def three(v, rows):
    lane = lax.broadcasted_iota(jnp.int32, (rows, 128), 1)
    v = jnp.broadcast_to(v, (rows, 128))
    hi = v.astype(BF16).astype(F32)
    mid = (v - hi).astype(BF16).astype(F32)
    lo = v - hi - mid
    return jnp.where(lane == 0, hi, jnp.where(lane == 1, mid, jnp.where(lane == 2, lo, 0.0))).astype(BF16)


def kernel(
    p_ref, q_ref, c_ref, pat_ref, off_ref, out_ref, loss_ref,
    G, E, S, CQ, C2, NB, acc, rb1, nar, rb2n, rb2, own, cv, qv, patv, offv, patb, st_s, st_r, rs_r,
    qs, qr, qp_s, qp_r,
    az_ss, az_rs, bz_ss, bz_rs, ax_ss, ax_rs, bx_ss, bx_rs, q_ss, q_rs, st_ss, st_rs, rs_ss, rs_rs,
    n1_ss, n1_rs, n2_ss, n2_rs, c_ss, c_rs, qp_ss, qp_rs, loc,
):
    dp = lax.axis_index("dp")
    me = lax.axis_index("cent")
    x, z = me // NZ, me % NZ
    y, core = dp // 2, dp % 2
    sib = (dp + 1 - 2 * core, me)
    z4 = (z + NZ // 2) % NZ

    def cdev(xx, zz):
        return (dp, xx * NZ + zz)

    loads = [
        pltpu.make_async_copy(src, dst, loc.at[i])
        for i, (src, dst) in enumerate(
            [(p_ref, G.at[z, x]), (q_ref, qv), (c_ref, cv), (pat_ref, patv), (off_ref, offv)]
        )
    ]
    for cp in loads:
        cp.start()

    barrier = pltpu.get_barrier_semaphore()
    for dev in (
        cdev(x, (z + 1) % NZ), cdev(x, (z + NZ - 1) % NZ),
        cdev((x + 1) % NX, z), cdev((x + 2) % NX, z), cdev((x + 3) % NX, z),
    ):
        pl.semaphore_signal(barrier, inc=1, device_id=dev, device_id_type=MESH)
    for o in range(1, DP):
        pl.semaphore_signal(barrier, inc=1, device_id=((dp + o) % DP, me), device_id_type=MESH)
    loads[1].wait()
    qs[...] = jnp.zeros_like(qs)
    qs[0:4, :] = qv[...].astype(F32)
    qr[dp] = qs[...]
    loads[0].wait()
    pl.semaphore_wait(barrier, 5 + DP - 1)

    def q_copy(o, src):
        return rcopy(qs, qr.at[src], q_ss.at[o], q_rs.at[src], ((dp + o) % DP, me))

    def zdev(step):
        return (dp, x * NZ + (z + NZ + step) % NZ)

    def xdev(step):
        return (dp, ((x + NX + step) % NX) * NZ + z)

    STEP = (1, -1)

    def a_z(zs, side, part=None):
        lo, n = (0, D) if part is None else (part * HD, HD)
        ref = G.at[zs, x, pl.ds(0, RA), pl.ds(lo, n)]
        return rcopy(ref, ref, az_ss.at[zs, side], az_rs.at[zs if part != 1 else NZ], zdev(STEP[side]))

    def b_z(zs, side, part):
        ref = G.at[zs, pl.ds(part * (NX // 2), NX // 2), pl.ds(RA, RB)]
        return rcopy(ref, ref, bz_ss.at[zs, side, part], bz_rs.at[zs, part], zdev(STEP[side]))

    def a_x(zs, xs, side):
        ref = G.at[zs, xs, pl.ds(0, RA)]
        return rcopy(ref, ref, ax_ss.at[zs, side], ax_rs.at[zs, side], xdev(STEP[side]))

    def a_x2(zs, xs, side):
        ref = G.at[zs, xs, pl.ds(0, RA), pl.ds(side * HD, HD)]
        return rcopy(ref, ref, ax_ss.at[zs, 2 + side], ax_rs.at[zs, 2 + side], xdev(STEP[side]))

    def b_x(xs, i):
        ref = G.at[z, xs, pl.ds(RA, RB)]
        return rcopy(ref, ref, bx_ss.at[i], bx_rs.at[i], xdev(i))

    def xfrom(side, n=1):
        return (x + NX - n * STEP[side]) % NX

    def zfrom(side, n):
        return (z + NZ - n * STEP[side]) % NZ

    def send_ax(zs):
        for side in range(2):
            a_x(zs, x, side).start()

    def hop_ax(zs):
        for side in range(2):
            a_x(zs, xfrom(side), side).wait_recv()
            a_x2(zs, xfrom(side), side).start()

    def end_ax(zs):
        for side in range(2):
            a_x2(zs, xfrom(side, 2), side).wait_recv()

    def take_a(d):
        for side in range(2):
            zs = zfrom(side, d)
            if d < 4:
                a_z(zs, side).wait_recv()
                a_z(zs, side, None if d < 3 else side).start()
                send_ax(zs)
            else:
                a_z(zs, side, side).wait_recv()
        if d == 4:
            send_ax(zfrom(0, 4))

    def take_b(d, part):
        for side in range(2):
            zs = zfrom(side, d)
            if d < 4:
                b_z(zs, side, part).wait_recv()
                if d < 3 or part == side:
                    b_z(zs, side, part).start()
            elif part == side:
                b_z(zs, side, part).wait_recv()

    def hop(d):
        for side in range(2 if 0 < d < 4 else 1):
            hop_ax(zfrom(side, d))

    def end(d):
        for side in range(2 if 0 < d < 4 else 1):
            end_ax(zfrom(side, d))

    def gather(compute):
        for side in range(2):
            a_z(z, side).start()
        for i in (2, 1, 3):
            b_x(x, i).start()
        send_ax(z)
        for o in range(1, DP):
            q_copy(o, dp).start()
        take_a(1)
        for i in (1, 3, 2):
            b_x((x + NX - i) % NX, i).wait_recv()
        for part in range(2):
            for side in range(2):
                b_z(z, side, part).start()
        take_a(2)
        hop(0)
        early()
        take_b(1, 0)
        take_b(1, 1)
        hop(1)
        hop(2)
        take_a(3)
        take_b(2, 0)
        take_b(2, 1)
        take_a(4)
        take_b(3, 0)
        end(1)
        hop(3)
        end(0)
        compute(0)
        end(2)
        compute(1)
        take_b(3, 1)
        hop(4)
        compute(2)
        end(3)
        compute(3)
        take_b(4, 0)
        take_b(4, 1)
        end(4)
        compute(4)

    def gather_drain():
        for i in range(1, NX):
            b_x(x, i).wait_send()
        for side in range(2):
            for d in range(4):
                zs = zfrom(side, d)
                a_z(zs, side, None if d < 3 else side).wait_send()
                for part in range(2):
                    if d < 3 or part == side:
                        b_z(zs, side, part).wait_send()

        def w(zs, _):
            for side in range(2):
                a_x(zs, x, side).wait_send()
                a_x2(zs, xfrom(side), side).wait_send()
            return 0

        lax.fori_loop(0, NZ, w, 0)

    def q_wait(o, _):
        q_copy(o, (dp + DP - o) % DP).wait_recv()
        return 0

    def early():
        for i in range(2, 5):
            loads[i].wait()
        c0 = cv[...]
        CQ[0:KL, :] = c0.astype(BF16)
        NB[...] = jnp.broadcast_to(jnp.sum(c0 * c0, axis=1, keepdims=True), (KL, 128))
        lane = lax.broadcasted_iota(jnp.int32, (8, BLOCK), 1)
        sub = lax.broadcasted_iota(jnp.int32, (8, BLOCK), 0)
        pick = (lane == me * 4 + sub) & (sub < 4)
        for j in range(DP):
            for i in range(5):
                row = patv[i:i + 1, j * BLOCK:(j + 1) * BLOCK] if i < 4 else offv[j:j + 1, :]
                vals = jnp.where(pick, jnp.broadcast_to(row.astype(F32), (8, BLOCK)), 0.0)
                patb[i, 8 * j:8 * j + 8, :] = jnp.broadcast_to(jnp.sum(vals, axis=1, keepdims=True), (8, BLOCK))
        lax.fori_loop(1, DP, q_wait, 0)
        CQ[KL:KL + QP, :] = qr[...].reshape(QP, D).astype(BF16)

    def column(k):
        d = (k + 1) // 2
        sgn = 1 - 2 * (k % 2)
        return (z + NZ + sgn * d) % NZ

    def st_copy(it, xc, zc, xs, zs):
        return rcopy(
            st_s.at[zc * NX + xc], st_r.at[it, zs * NX + xs], st_ss.at[it], st_rs.at[it],
            cdev(xc, (zc + NZ // 2) % NZ),
        )

    def dot_nt(lhs, rhs):
        return lax.dot_general(lhs, rhs, (((1,), (1,)), ((), ())), preferred_element_type=F32)

    def ship(it, zc, mine):
        if mine:
            st_r[it, z * NX + x] = st_s[z4 * NX + x]
            for i in range(1, NX):
                st_copy(it, (x + i) % NX, z4, x, z).start()
        else:
            for xc in range(NX):
                st_copy(it, xc, zc, x, z).start()

    def columns(it, zcs):
        for zc in zcs:
            lhs = CQ[...] if it == 0 else C2[:, 0:D]
            dots = dot_nt(lhs, G[zc].reshape(NX * BLOCK, D))
            nb = NB[...]
            for xc in range(NX):
                a = xc * BLOCK
                ll = sharpness * (2.0 * dots[0:KL, a:a + BLOCK] - nb)
                m = jnp.max(ll, axis=0, keepdims=True)
                e = jnp.exp(ll - m)
                E[zc, :, a:a + BLOCK] = e
                st_s[zc * NX + xc, 0:1, :] = m
                st_s[zc * NX + xc, 1:2, :] = jnp.sum(e, axis=0, keepdims=True)
            if it == 0:
                S[zc] = dots[KL:KL + QP, :] * sharpness

    def softmax_first():
        def compute(d):
            zcs = [zfrom(side, d) for side in range(2 if 0 < d < 4 else 1)]
            columns(0, zcs)
            for zc in zcs:
                ship(0, zc, d == 4)

        gather(compute)

    def softmax_second():
        for h in range(CH):
            rows_wait(0, h)
        NB[...] = jnp.broadcast_to(jnp.sum(C2[:, D:W].astype(F32), axis=1, keepdims=True), (KL, 128))
        for grp in (FAR, NEAR):
            columns(1, [column(k) for k in grp])
            for k in grp:
                ship(1, column(k), k == 7)

    def rs_copy(it, dx, dz):
        ref = rs_r.at[it, z4 * NX + x]
        far = 1 if dz in (3, 4, 5, 6) else 0
        return rcopy(ref, ref, rs_ss.at[it], rs_rs.at[it, far], cdev((x + dx) % NX, (z + dz) % NZ))

    def all_of(ref, n, ss, rs):
        some = ref.at[pl.ds(0, n)]
        return rcopy(some, some, ss, rs, sib)

    def owner_combine(it):
        all_of(st_r.at[it], CENT - 1, st_ss.at[it], st_rs.at[it]).wait_recv()
        m = st_r[it, :, 0:1, :]
        s = st_r[it, :, 1:2, :]
        top = jnp.max(m, axis=0)
        tot = jnp.sum(s * jnp.exp(m - top[None]), axis=0)
        rs_r[it, z4 * NX + x, 0:1, :] = top
        rs_r[it, z4 * NX + x, 1:2, :] = 1.0 / tot
        for dz in (4, 3, 5, 6, 2, 1, 7, 0):
            for dx in (2, 1, 3, 0):
                if dz or dx:
                    rs_copy(it, dx, dz).start()

    def query_post():
        pats = [patb[i] for i in range(4)]
        off = patb[4]
        lane = lax.broadcasted_iota(jnp.int32, (QP, BLOCK), 1)
        lanef = lane.astype(F32)

        def allow_of(b):
            return (pats[0] == b) | (pats[1] == b) | (pats[2] == b) | (pats[3] == b)

        def p1(zc, mx):
            for xc in range(NX):
                b = (dp * CENT + xc * NZ + zc).astype(F32)
                sv = S[zc, :, xc * BLOCK:(xc + 1) * BLOCK]
                mx = jnp.maximum(mx, jnp.where(allow_of(b), sv, NEG))
            return mx

        mx = lax.fori_loop(0, NZ, p1, jnp.full((QP, BLOCK), NEG, F32))
        mrow = jnp.max(mx, axis=1, keepdims=True)
        mb = jnp.broadcast_to(mrow, (QP, BLOCK))

        def p2(zc, carry):
            tot, pos = carry
            for xc in range(NX):
                b = (dp * CENT + xc * NZ + zc).astype(F32)
                sv = S[zc, :, xc * BLOCK:(xc + 1) * BLOCK]
                tot = tot + jnp.where(allow_of(b), jnp.exp(sv - mb), 0.0)
                pos = pos + jnp.where((pats[0] == b) & (lanef == off), sv, 0.0)
            return tot, pos

        zero = jnp.zeros((QP, BLOCK), F32)
        tot, pos = lax.fori_loop(0, NZ, p2, (zero, zero))
        trow = jnp.broadcast_to(jnp.sum(tot, axis=1, keepdims=True), (QP, BLOCK))
        prow = jnp.broadcast_to(jnp.sum(pos, axis=1, keepdims=True), (QP, BLOCK))
        packed = jnp.where(lane == 0, mb, jnp.where(lane == 1, trow, prow))
        qp_s[...] = packed.reshape(DP, 8, BLOCK)
        qp_r[dp] = qp_s[dp]

        def snd(o, _):
            qp_copy(o, (dp + o) % DP, dp).start()
            return 0

        lax.fori_loop(1, DP, snd, 0)

    def qp_copy(o, dst, src):
        return rcopy(qp_s.at[dst], qp_r.at[src], qp_ss.at[o], qp_rs.at[src], (dst, me))

    def query_finish():
        def w(o, _):
            qp_copy(o, (dp + o) % DP, (dp + o) % DP).wait_recv()
            return 0

        lax.fori_loop(1, DP, w, 0)
        m = qp_r[:, :, 0:1]
        t = qp_r[:, :, 1:2]
        p = qp_r[:, :, 2:3]
        top = jnp.max(m, axis=0)
        tot = jnp.sum(t * jnp.exp(m - top[None]), axis=0)
        ps = jnp.sum(p, axis=0)
        loss = jnp.broadcast_to(jnp.log(tot) + top - ps, (8, BLOCK))
        lane = lax.broadcasted_iota(jnp.int32, (8, BLOCK), 1)
        sub = lax.broadcasted_iota(jnp.int32, (8, BLOCK), 0)
        loss_ref[...] = jnp.sum(jnp.where(lane == sub, loss, 0.0), axis=0, keepdims=True)[:, 0:4]

        def ws(o, _):
            qp_copy(o, (dp + o) % DP, dp).wait_send()
            return 0

        lax.fori_loop(1, DP, ws, 0)

    def stats_wait(it, grp):
        n, far = (16, 1) if grp is FAR else (15, 0)
        all_of(rs_r.at[it], n, rs_ss.at[it], rs_rs.at[it, far]).wait_recv()

    def stats_drain(it):
        all_of(st_r.at[it], CENT - 1, st_ss.at[it], st_rs.at[it]).wait_send()
        all_of(rs_r.at[it], CENT - 1, rs_ss.at[it], rs_rs.at[it, 0]).wait_send()

    def numer(it, h, grp):
        rows = pl.ds(pl.multiple_of(h * RC, RC), RC)
        cnt = jnp.zeros((RC, BLOCK), F32)
        tot = jnp.zeros((RC, D), F32)
        for k in grp:
            zc = column(k)
            parts = []
            for xc in range(NX):
                a = xc * BLOCK
                g = jnp.exp(st_s[zc * NX + xc, 0:1, :] - rs_r[it, zc * NX + xc, 0:1, :]) * rs_r[it, zc * NX + xc, 1:2, :]
                r = E[zc, rows, a:a + BLOCK] * g
                cnt = cnt + r
                parts.append(r.astype(BF16))
            tot = tot + jnp.dot(
                jnp.concatenate(parts, axis=1), G[zc].reshape(NX * BLOCK, D), preferred_element_type=F32
            )
        if grp is NEAR:
            acc[it, rows, 0:D] = tot
            acc[it, rows, D:W] = cnt
        else:
            acc[it, rows, 0:D] += tot
            acc[it, rows, D:W] += cnt

    mine_at = [pl.multiple_of(h * RC + core * RH, RH) for h in range(CH)]
    theirs_at = [pl.multiple_of(h * RC + RH - core * RH, RH) for h in range(CH)]

    def pair_copy(it, h):
        return rcopy(acc.at[it, pl.ds(pl.multiple_of(h * RC + RH - core * RH, RH), RH)], rb1.at[it, h], n1_ss.at[it, h], n1_rs.at[it, h], sib)

    def quarter(h, yy):
        return pl.ds(pl.multiple_of(h * RC + core * RH + yy * RQ, RQ), RQ)

    def y_copy(it, h, i):
        yp = (y + i) % NY
        sem = (n2_ss.at[it, h, i], n2_rs.at[it, h, i])
        if NARROW[it]:
            src = nar.at[it, h, pl.ds(pl.multiple_of(yp * RQ, RQ), RQ)]
            return rcopy(src, rb2n.at[it, h, i], *sem, (yp * 2 + core, me))
        return rcopy(acc.at[it, quarter(h, yp)], rb2.at[it, h, i], *sem, (yp * 2 + core, me))

    def pair_sum(it, h):
        pair_copy(it, h).wait_recv()
        tot = acc[it, pl.ds(mine_at[h], RH), :] + rb1[it, h]
        acc[it, pl.ds(mine_at[h], RH), :] = tot
        if NARROW[it]:
            nar[it, h, :, 0:D] = tot[:, 0:D].astype(BF16)
            nar[it, h, :, D:W] = three(jnp.sum(tot[:, D:W], axis=1, keepdims=True), RH)
        for i in (2, 1, 3):
            y_copy(it, h, i).start()

    def update(it, h):
        tot = acc[it, quarter(h, y), :]
        for i in (1, 3, 2):
            y_copy(it, h, i).wait_recv()
            tot = tot + (rb2n[it, h, i].astype(F32) if NARROW[it] else rb2[it, h, i])
        counts = jnp.sum(tot[:, D:W], axis=1, keepdims=True)
        cold = cv[quarter(h, y), :] if it == 0 else own[h]
        return (tot[:, 0:D] + cold) / (counts + 1.0)

    def row_copy(k, h, i):
        arr = C2 if k == 0 else out_ref
        ref = arr.at[quarter(h, y)]
        return rcopy(ref, ref, c_ss.at[k, h, i], c_rs.at[k, h, i], (((y + i) % NY) * 2 + core, me))

    def half_copy(k, h):
        arr = C2 if k == 0 else out_ref
        ref = arr.at[pl.ds(mine_at[h], RH)]
        return rcopy(ref, ref, c_ss.at[k, h, 0], c_rs.at[k, h, 0], sib)

    def rows_send(k, h):
        for i in (2, 1, 3):
            row_copy(k, h, i).start()

    def rows_pass(k, h):
        for i in (1, 3, 2):
            row_copy(k, h, i).wait_recv()
        half_copy(k, h).start()

    def rows_wait(k, h):
        half_copy(k, h).wait_recv()

    def reduce_drain(it):
        for h in range(CH):
            pair_copy(it, h).wait_send()
            for i in range(1, NY):
                y_copy(it, h, i).wait_send()
                row_copy(it, h, i).wait_send()
            half_copy(it, h).wait_send()

    def finish():
        if STOP < 1:
            early_drain()
        if STOP < 90:
            out_ref[...] = jnp.zeros_like(out_ref)
            loss_ref[...] = jnp.zeros_like(loss_ref)

    def early_drain():
        if STOP >= 0:
            gather_drain()

        def wsq(o, _):
            q_copy(o, dp).wait_send()
            return 0

        lax.fori_loop(1, DP, wsq, 0)

    def mid(it):
        stats_wait(it, NEAR)
        def near(h, _):
            numer(it, h, NEAR)
            return 0

        lax.fori_loop(0, CH, near, 0)
        stats_wait(it, FAR)
        def far(h, _):
            numer(it, h, FAR)
            pair_copy(it, h).start()
            return 0

        lax.fori_loop(0, CH, far, 0)
        for h in range(CH):
            pair_sum(it, h)

    if STOP == -2:
        for o in range(1, DP):
            q_copy(o, dp).start()
        lax.fori_loop(1, DP, q_wait, 0)
        for i in range(2, 5):
            loads[i].wait()
        return finish()
    if STOP == -1:
        for o in range(1, DP):
            q_copy(o, dp).start()
        early()
        return finish()
    if STOP == 0:
        gather(lambda d: None)
        return finish()
    softmax_first()
    owner_combine(0)
    early_drain()
    if STOP == 1:
        stats_wait(0, NEAR)
        stats_wait(0, FAR)
        stats_drain(0)
        return finish()
    query_post()
    if STOP == 2:
        stats_wait(0, NEAR)
        stats_wait(0, FAR)
        stats_drain(0)
        query_finish()
        return finish()
    mid(0)
    for h in range(CH):
        newc = update(0, h)
        own[h] = newc
        C2[quarter(h, y), 0:D] = newc.astype(BF16)
        C2[quarter(h, y), D:W] = three(jnp.sum(newc * newc, axis=1, keepdims=True), RQ)
        rows_send(0, h)
    stats_drain(0)
    for h in range(CH):
        rows_pass(0, h)
    if STOP == 5:
        for h in range(CH):
            rows_wait(0, h)
        reduce_drain(0)
        query_finish()
        return finish()

    softmax_second()
    owner_combine(1)
    query_finish()
    if STOP == 6:
        stats_wait(1, NEAR)
        stats_wait(1, FAR)
        stats_drain(1)
        reduce_drain(0)
        return finish()
    mid(1)
    for h in range(CH):
        out_ref[quarter(h, y), :] = update(1, h).astype(BF16)
        rows_send(1, h)
    stats_drain(1)
    reduce_drain(0)
    for h in range(CH):
        rows_pass(1, h)
    for h in range(CH):
        rows_wait(1, h)
    reduce_drain(1)
    finish()


def on_device(passages, queries, init_centroids, pattern, positive_offset):
    vm = pl.BlockSpec(memory_space=pltpu.VMEM)
    anywhere = pl.BlockSpec(memory_space=pl.ANY)
    dma = pltpu.SemaphoreType.DMA
    centroids, loss = pl.pallas_call(
        kernel,
        out_shape=(jax.ShapeDtypeStruct((KL, D), BF16), jax.ShapeDtypeStruct((1, 4), F32)),
        in_specs=[anywhere] * 5,
        out_specs=(vm, vm),
        scratch_shapes=[
            pltpu.VMEM((NZ, NX, BLOCK, D), BF16),
            pltpu.VMEM((NZ, KL, NX * BLOCK), F32),
            pltpu.VMEM((NZ, QP, NX * BLOCK), F32),
            pltpu.VMEM((KL + QP, D), BF16),
            pltpu.VMEM((KL, W), BF16),
            pltpu.VMEM((KL, 128), F32),
            pltpu.VMEM((2, KL, W), F32),
            pltpu.VMEM((2, CH, RH, W), F32),
            pltpu.VMEM((2, CH, RH, W), BF16),
            pltpu.VMEM((2, CH, NY, RQ, W), BF16),
            pltpu.VMEM((2, CH, NY, RQ, W), F32),
            pltpu.VMEM((CH, RQ, D), F32),
            pltpu.VMEM((KL, D), F32),
            pltpu.VMEM((4, D), BF16),
            pltpu.VMEM((4, 1024), jnp.int32),
            pltpu.VMEM((DP, 128), jnp.int32),
            pltpu.VMEM((5, QP, 128), F32),
            pltpu.VMEM((CENT, 2, 128), F32),
            pltpu.VMEM((2, CENT, 2, 128), F32),
            pltpu.VMEM((2, CENT, 2, 128), F32),
            pltpu.VMEM((8, D), F32),
            pltpu.VMEM((DP, 8, D), F32),
            pltpu.VMEM((DP, 8, 128), F32),
            pltpu.VMEM((DP, 8, 128), F32),
            dma((NZ, 2)), dma((NZ + 1,)), dma((NZ, 2, 2)), dma((NZ, 2)),
            dma((NZ, 4)), dma((NZ, 4)), dma((4,)), dma((4,)),
            dma((DP,)), dma((DP,)),
            dma((2,)), dma((2,)),
            dma((2,)), dma((2, 2)),
            dma((2, CH)), dma((2, CH)),
            dma((2, CH, NY)), dma((2, CH, NY)),
            dma((2, CH, NY)), dma((2, CH, NY)),
            dma((DP,)), dma((DP,)),
            dma((5,)),
        ],
        compiler_params=pltpu.CompilerParams(
            collective_id=0, has_side_effects=True, vmem_limit_bytes=56 * 1024 * 1024
        ),
    )(passages, queries, init_centroids, pattern.T, positive_offset.reshape(DP, 128))
    return centroids.astype(F32), loss.reshape(4)


def solution(mesh):
    placed = (P(("dp", "cent"), None), P(("dp", "cent"), None), P("cent", None), P(), P())
    return jax.shard_map(
        on_device,
        mesh=mesh,
        in_specs=placed,
        out_specs=(P("cent", None), P(("dp", "cent"))),
        check_vma=False,
    )
```

```python
import jax
import jax.numpy as jnp
from jax import lax
from jax.experimental import pallas as pl
from jax.experimental.pallas import tpu as pltpu
from jax.sharding import PartitionSpec as P

MESH = pl.DeviceIdType.MESH
BLOCK = 128
D = 768
HD = 384
NX, NZ, NY = 4, 8, 4
CENT = NX * NZ
DP = 2 * NY
KL = 256
QP = 64
W = D + 128
CH = 2
RC = KL // CH
RH = RC // 2
RQ = RH // NY
sharpness = 0.05
NEG = -1e30
STOP = 99
RA = 80
RB = 128 - RA
NARROW = (True, True)
FAR, NEAR = (0, 1, 2, 3), (4, 5, 6, 7)
F32 = jnp.float32
BF16 = jnp.bfloat16


def rcopy(src, dst, ss, rs, dev):
    return pltpu.make_async_remote_copy(
        src_ref=src, dst_ref=dst, send_sem=ss, recv_sem=rs, device_id=dev, device_id_type=MESH
    )


def three(v, rows):
    lane = lax.broadcasted_iota(jnp.int32, (rows, 128), 1)
    v = jnp.broadcast_to(v, (rows, 128))
    hi = v.astype(BF16).astype(F32)
    mid = (v - hi).astype(BF16).astype(F32)
    lo = v - hi - mid
    return jnp.where(lane == 0, hi, jnp.where(lane == 1, mid, jnp.where(lane == 2, lo, 0.0))).astype(BF16)


def kernel(
    p_ref, q_ref, c_ref, pat_ref, off_ref, out_ref, loss_ref,
    G, E, S, CQ, C2, NB, acc, rb1, nar, rb2n, rb2, own, cv, qv, patv, offv, patb, st_s, st_r, rs_r,
    qs, qr, qp_s, qp_r,
    az_ss, az_rs, bz_ss, bz_rs, ax_ss, ax_rs, bx_ss, bx_rs, q_ss, q_rs, st_ss, st_rs, rs_ss, rs_rs,
    n1_ss, n1_rs, n2_ss, n2_rs, c_ss, c_rs, qp_ss, qp_rs, loc,
):
    dp = lax.axis_index("dp")
    me = lax.axis_index("cent")
    x, z = me // NZ, me % NZ
    y, core = dp // 2, dp % 2
    sib = (dp + 1 - 2 * core, me)
    z4 = (z + NZ // 2) % NZ

    def cdev(xx, zz):
        return (dp, xx * NZ + zz)

    loads = [
        pltpu.make_async_copy(src, dst, loc.at[i])
        for i, (src, dst) in enumerate(
            [(p_ref, G.at[z, x]), (q_ref, qv), (c_ref, cv), (pat_ref, patv), (off_ref, offv)]
        )
    ]
    for cp in loads:
        cp.start()

    barrier = pltpu.get_barrier_semaphore()
    for dev in (
        cdev(x, (z + 1) % NZ), cdev(x, (z + NZ - 1) % NZ),
        cdev((x + 1) % NX, z), cdev((x + 2) % NX, z), cdev((x + 3) % NX, z),
    ):
        pl.semaphore_signal(barrier, inc=1, device_id=dev, device_id_type=MESH)
    for o in range(1, DP):
        pl.semaphore_signal(barrier, inc=1, device_id=((dp + o) % DP, me), device_id_type=MESH)
    loads[1].wait()
    qs[...] = jnp.zeros_like(qs)
    qs[0:4, :] = qv[...].astype(F32)
    qr[dp] = qs[...]
    loads[0].wait()
    pl.semaphore_wait(barrier, 5 + DP - 1)

    def q_copy(o, src):
        return rcopy(qs, qr.at[src], q_ss.at[o], q_rs.at[src], ((dp + o) % DP, me))

    def zdev(step):
        return (dp, x * NZ + (z + NZ + step) % NZ)

    def xdev(step):
        return (dp, ((x + NX + step) % NX) * NZ + z)

    STEP = (1, -1)

    def a_z(zs, side, part=None):
        lo, n = (0, D) if part is None else (part * HD, HD)
        ref = G.at[zs, x, pl.ds(0, RA), pl.ds(lo, n)]
        return rcopy(ref, ref, az_ss, az_rs.at[zs if part != 1 else NZ], zdev(STEP[side]))

    def b_z(zs, side, part):
        ref = G.at[zs, pl.ds(part * (NX // 2), NX // 2), pl.ds(RA, RB)]
        return rcopy(ref, ref, bz_ss, bz_rs.at[zs, part], zdev(STEP[side]))

    def a_x(zs, xs, side):
        ref = G.at[zs, xs, pl.ds(0, RA)]
        return rcopy(ref, ref, ax_ss.at[0], ax_rs.at[zs, side], xdev(STEP[side]))

    def a_x2(zs, xs, side):
        ref = G.at[zs, xs, pl.ds(0, RA), pl.ds(side * HD, HD)]
        return rcopy(ref, ref, ax_ss.at[1], ax_rs.at[zs, 2 + side], xdev(STEP[side]))

    def b_x(xs, i):
        ref = G.at[z, xs, pl.ds(RA, RB)]
        return rcopy(ref, ref, bx_ss.at[i], bx_rs.at[i], xdev(i))

    def xfrom(side, n=1):
        return (x + NX - n * STEP[side]) % NX

    def zfrom(side, n):
        return (z + NZ - n * STEP[side]) % NZ

    def send_ax(zs):
        for side in range(2):
            a_x(zs, x, side).start()

    def hop_ax(zs):
        for side in range(2):
            a_x(zs, xfrom(side), side).wait_recv()
            a_x2(zs, xfrom(side), side).start()

    def end_ax(zs):
        for side in range(2):
            a_x2(zs, xfrom(side, 2), side).wait_recv()

    def take_a(d):
        for side in range(2):
            zs = zfrom(side, d)
            if d < 4:
                a_z(zs, side).wait_recv()
                a_z(zs, side, None if d < 3 else side).start()
                send_ax(zs)
            else:
                a_z(zs, side, side).wait_recv()
        if d == 4:
            send_ax(zfrom(0, 4))

    def take_b(d, part):
        for side in range(2):
            zs = zfrom(side, d)
            if d < 4:
                b_z(zs, side, part).wait_recv()
                if d < 3 or part == side:
                    b_z(zs, side, part).start()
            elif part == side:
                b_z(zs, side, part).wait_recv()

    def hop(d):
        for side in range(2 if 0 < d < 4 else 1):
            hop_ax(zfrom(side, d))

    def end(d):
        for side in range(2 if 0 < d < 4 else 1):
            end_ax(zfrom(side, d))

    def gather(compute):
        for side in range(2):
            a_z(z, side).start()
        for i in (2, 1, 3):
            b_x(x, i).start()
        send_ax(z)
        for o in range(1, DP):
            q_copy(o, dp).start()
        take_a(1)
        for i in (1, 3, 2):
            b_x((x + NX - i) % NX, i).wait_recv()
        for part in range(2):
            for side in range(2):
                b_z(z, side, part).start()
        take_a(2)
        hop(0)
        early()
        take_b(1, 0)
        take_b(1, 1)
        hop(1)
        hop(2)
        take_a(3)
        take_b(2, 0)
        take_b(2, 1)
        take_a(4)
        take_b(3, 0)
        end(1)
        hop(3)
        end(0)
        compute(0)
        end(2)
        compute(1)
        take_b(3, 1)
        hop(4)
        compute(2)
        end(3)
        compute(3)
        take_b(4, 0)
        take_b(4, 1)
        end(4)
        compute(4)

    def gather_drain():
        for i in range(1, NX):
            b_x(x, i).wait_send()

        def wait_all(ref, ss):
            rcopy(ref, ref, ss, bx_rs.at[0], sib).wait_send()

        flat = G.at[:, :, pl.ds(0, RA)]
        wait_all(flat.at[0, pl.ds(0, 1)], az_ss)
        wait_all(flat.at[pl.ds(0, 3), pl.ds(0, 2)], az_ss)
        wait_all(G.at[pl.ds(0, 7), :, pl.ds(RA, RB)], bz_ss)
        wait_all(flat.at[pl.ds(0, 4)], ax_ss.at[0])
        wait_all(flat.at[pl.ds(0, 2)], ax_ss.at[1])

    def q_wait(o, _):
        q_copy(o, (dp + DP - o) % DP).wait_recv()
        return 0

    def early():
        for i in range(2, 5):
            loads[i].wait()
        c0 = cv[...]
        CQ[0:KL, :] = c0.astype(BF16)
        NB[...] = jnp.broadcast_to(jnp.sum(c0 * c0, axis=1, keepdims=True), (KL, 128))
        lane = lax.broadcasted_iota(jnp.int32, (8, BLOCK), 1)
        sub = lax.broadcasted_iota(jnp.int32, (8, BLOCK), 0)
        pick = (lane == me * 4 + sub) & (sub < 4)
        for j in range(DP):
            for i in range(5):
                row = patv[i:i + 1, j * BLOCK:(j + 1) * BLOCK] if i < 4 else offv[j:j + 1, :]
                vals = jnp.where(pick, jnp.broadcast_to(row.astype(F32), (8, BLOCK)), 0.0)
                patb[i, 8 * j:8 * j + 8, :] = jnp.broadcast_to(jnp.sum(vals, axis=1, keepdims=True), (8, BLOCK))
        for o in range(1, DP):
            q_wait(o, 0)
        CQ[KL:KL + QP, :] = qr[...].reshape(QP, D).astype(BF16)

    def column(k):
        d = (k + 1) // 2
        sgn = 1 - 2 * (k % 2)
        return (z + NZ + sgn * d) % NZ

    def st_copy(it, xc, zc, xs, zs):
        return rcopy(
            st_s.at[zc * NX + xc], st_r.at[it, zs * NX + xs], st_ss.at[it], st_rs.at[it],
            cdev(xc, (zc + NZ // 2) % NZ),
        )

    def dot_nt(lhs, rhs):
        return lax.dot_general(lhs, rhs, (((1,), (1,)), ((), ())), preferred_element_type=F32)

    def ship(it, zc, mine):
        if mine:
            st_r[it, z * NX + x] = st_s[z4 * NX + x]
            for i in range(1, NX):
                st_copy(it, (x + i) % NX, z4, x, z).start()
        else:
            for xc in range(NX):
                st_copy(it, xc, zc, x, z).start()

    def columns(it, zcs):
        for zc in zcs:
            lhs = CQ[...] if it == 0 else C2[:, 0:D]
            dots = dot_nt(lhs, G[zc].reshape(NX * BLOCK, D))
            nb = NB[...]
            for xc in range(NX):
                a = xc * BLOCK
                ll = sharpness * (2.0 * dots[0:KL, a:a + BLOCK] - nb)
                m = jnp.max(ll, axis=0, keepdims=True)
                e = jnp.exp(ll - m)
                E[zc, :, a:a + BLOCK] = e
                st_s[zc * NX + xc, 0:1, :] = m
                st_s[zc * NX + xc, 1:2, :] = jnp.sum(e, axis=0, keepdims=True)
            if it == 0:
                S[zc] = dots[KL:KL + QP, :] * sharpness

    def softmax_first():
        def compute(d):
            zcs = [zfrom(side, d) for side in range(2 if 0 < d < 4 else 1)]
            columns(0, zcs)
            for zc in zcs:
                ship(0, zc, d == 4)

        gather(compute)

    def softmax_second():
        for h in range(CH):
            rows_wait(0, h)
        NB[...] = jnp.broadcast_to(jnp.sum(C2[:, D:W].astype(F32), axis=1, keepdims=True), (KL, 128))
        for grp in (FAR, NEAR):
            columns(1, [column(k) for k in grp])
            for k in grp:
                ship(1, column(k), k == 7)

    def rs_copy(it, dx, dz):
        ref = rs_r.at[it, z4 * NX + x]
        far = 1 if dz in (3, 4, 5, 6) else 0
        return rcopy(ref, ref, rs_ss.at[it], rs_rs.at[it, far], cdev((x + dx) % NX, (z + dz) % NZ))

    def all_of(ref, n, ss, rs):
        some = ref.at[pl.ds(0, n)]
        return rcopy(some, some, ss, rs, sib)

    def owner_combine(it):
        all_of(st_r.at[it], CENT - 1, st_ss.at[it], st_rs.at[it]).wait_recv()
        m = st_r[it, :, 0:1, :]
        s = st_r[it, :, 1:2, :]
        top = jnp.max(m, axis=0)
        tot = jnp.sum(s * jnp.exp(m - top[None]), axis=0)
        rs_r[it, z4 * NX + x, 0:1, :] = top
        rs_r[it, z4 * NX + x, 1:2, :] = 1.0 / tot
        for dz in (4, 3, 5, 6, 2, 1, 7, 0):
            for dx in (2, 1, 3, 0):
                if dz or dx:
                    rs_copy(it, dx, dz).start()

    def query_post():
        pats = [patb[i] for i in range(4)]
        off = patb[4]
        lane = lax.broadcasted_iota(jnp.int32, (QP, BLOCK), 1)
        lanef = lane.astype(F32)

        def allow_of(b):
            return (pats[0] == b) | (pats[1] == b) | (pats[2] == b) | (pats[3] == b)

        def p1(zc, mx):
            for xc in range(NX):
                b = (dp * CENT + xc * NZ + zc).astype(F32)
                sv = S[zc, :, xc * BLOCK:(xc + 1) * BLOCK]
                mx = jnp.maximum(mx, jnp.where(allow_of(b), sv, NEG))
            return mx

        mx = lax.fori_loop(0, NZ, p1, jnp.full((QP, BLOCK), NEG, F32))
        mrow = jnp.max(mx, axis=1, keepdims=True)
        mb = jnp.broadcast_to(mrow, (QP, BLOCK))

        def p2(zc, carry):
            tot, pos = carry
            for xc in range(NX):
                b = (dp * CENT + xc * NZ + zc).astype(F32)
                sv = S[zc, :, xc * BLOCK:(xc + 1) * BLOCK]
                tot = tot + jnp.where(allow_of(b), jnp.exp(sv - mb), 0.0)
                pos = pos + jnp.where((pats[0] == b) & (lanef == off), sv, 0.0)
            return tot, pos

        zero = jnp.zeros((QP, BLOCK), F32)
        tot, pos = lax.fori_loop(0, NZ, p2, (zero, zero))
        trow = jnp.broadcast_to(jnp.sum(tot, axis=1, keepdims=True), (QP, BLOCK))
        prow = jnp.broadcast_to(jnp.sum(pos, axis=1, keepdims=True), (QP, BLOCK))
        packed = jnp.where(lane == 0, mb, jnp.where(lane == 1, trow, prow))
        qp_s[...] = packed.reshape(DP, 8, BLOCK)
        qp_r[dp] = qp_s[dp]

        def snd(o, _):
            qp_copy(o, (dp + o) % DP, dp).start()
            return 0

        lax.fori_loop(1, DP, snd, 0)

    def qp_copy(o, dst, src):
        return rcopy(qp_s.at[dst], qp_r.at[src], qp_ss.at[o], qp_rs.at[src], (dst, me))

    def query_finish():
        def w(o, _):
            qp_copy(o, (dp + o) % DP, (dp + o) % DP).wait_recv()
            return 0

        lax.fori_loop(1, DP, w, 0)
        m = qp_r[:, :, 0:1]
        t = qp_r[:, :, 1:2]
        p = qp_r[:, :, 2:3]
        top = jnp.max(m, axis=0)
        tot = jnp.sum(t * jnp.exp(m - top[None]), axis=0)
        ps = jnp.sum(p, axis=0)
        loss = jnp.broadcast_to(jnp.log(tot) + top - ps, (8, BLOCK))
        lane = lax.broadcasted_iota(jnp.int32, (8, BLOCK), 1)
        sub = lax.broadcasted_iota(jnp.int32, (8, BLOCK), 0)
        loss_ref[...] = jnp.sum(jnp.where(lane == sub, loss, 0.0), axis=0, keepdims=True)[:, 0:4]

        def ws(o, _):
            qp_copy(o, (dp + o) % DP, dp).wait_send()
            return 0

        lax.fori_loop(1, DP, ws, 0)

    def stats_wait(it, grp):
        n, far = (16, 1) if grp is FAR else (15, 0)
        all_of(rs_r.at[it], n, rs_ss.at[it], rs_rs.at[it, far]).wait_recv()

    def stats_drain(it):
        all_of(st_r.at[it], CENT - 1, st_ss.at[it], st_rs.at[it]).wait_send()
        all_of(rs_r.at[it], CENT - 1, rs_ss.at[it], rs_rs.at[it, 0]).wait_send()

    def numer(it, h, grp):
        rows = pl.ds(pl.multiple_of(h * RC, RC), RC)
        cnt = jnp.zeros((RC, BLOCK), F32)
        tot = jnp.zeros((RC, D), F32)
        for k in grp:
            zc = column(k)
            parts = []
            for xc in range(NX):
                a = xc * BLOCK
                g = jnp.exp(st_s[zc * NX + xc, 0:1, :] - rs_r[it, zc * NX + xc, 0:1, :]) * rs_r[it, zc * NX + xc, 1:2, :]
                r = E[zc, rows, a:a + BLOCK] * g
                cnt = cnt + r
                parts.append(r.astype(BF16))
            tot = tot + jnp.dot(
                jnp.concatenate(parts, axis=1), G[zc].reshape(NX * BLOCK, D), preferred_element_type=F32
            )
        if grp is NEAR:
            acc[it, rows, 0:D] = tot
            acc[it, rows, D:W] = cnt
        else:
            acc[it, rows, 0:D] += tot
            acc[it, rows, D:W] += cnt

    mine_at = [pl.multiple_of(h * RC + core * RH, RH) for h in range(CH)]
    theirs_at = [pl.multiple_of(h * RC + RH - core * RH, RH) for h in range(CH)]

    def pair_copy(it, h):
        return rcopy(acc.at[it, pl.ds(pl.multiple_of(h * RC + RH - core * RH, RH), RH)], rb1.at[it, h], n1_ss.at[it, h], n1_rs.at[it, h], sib)

    def quarter(h, yy):
        return pl.ds(pl.multiple_of(h * RC + core * RH + yy * RQ, RQ), RQ)

    def y_copy(it, h, i):
        yp = (y + i) % NY
        sem = (n2_ss.at[it, h, i], n2_rs.at[it, h, i])
        if NARROW[it]:
            src = nar.at[it, h, pl.ds(pl.multiple_of(yp * RQ, RQ), RQ)]
            return rcopy(src, rb2n.at[it, h, i], *sem, (yp * 2 + core, me))
        return rcopy(acc.at[it, quarter(h, yp)], rb2.at[it, h, i], *sem, (yp * 2 + core, me))

    def pair_sum(it, h):
        pair_copy(it, h).wait_recv()
        tot = acc[it, pl.ds(mine_at[h], RH), :] + rb1[it, h]
        acc[it, pl.ds(mine_at[h], RH), :] = tot
        if NARROW[it]:
            nar[it, h, :, 0:D] = tot[:, 0:D].astype(BF16)
            nar[it, h, :, D:W] = three(jnp.sum(tot[:, D:W], axis=1, keepdims=True), RH)
        for i in (2, 1, 3):
            y_copy(it, h, i).start()

    def update(it, h):
        tot = acc[it, quarter(h, y), :]
        for i in (1, 3, 2):
            y_copy(it, h, i).wait_recv()
            tot = tot + (rb2n[it, h, i].astype(F32) if NARROW[it] else rb2[it, h, i])
        counts = jnp.sum(tot[:, D:W], axis=1, keepdims=True)
        cold = cv[quarter(h, y), :] if it == 0 else own[h]
        return (tot[:, 0:D] + cold) / (counts + 1.0)

    def row_copy(k, h, i):
        arr = C2 if k == 0 else out_ref
        ref = arr.at[quarter(h, y)]
        return rcopy(ref, ref, c_ss.at[k, h, i], c_rs.at[k, h, i], (((y + i) % NY) * 2 + core, me))

    def half_copy(k, h):
        arr = C2 if k == 0 else out_ref
        ref = arr.at[pl.ds(mine_at[h], RH)]
        return rcopy(ref, ref, c_ss.at[k, h, 0], c_rs.at[k, h, 0], sib)

    def rows_send(k, h):
        for i in (2, 1, 3):
            row_copy(k, h, i).start()

    def rows_pass(k, h):
        for i in (1, 3, 2):
            row_copy(k, h, i).wait_recv()
        half_copy(k, h).start()

    def rows_wait(k, h):
        half_copy(k, h).wait_recv()

    def reduce_drain(it):
        for h in range(CH):
            pair_copy(it, h).wait_send()
            for i in range(1, NY):
                y_copy(it, h, i).wait_send()
                row_copy(it, h, i).wait_send()
            half_copy(it, h).wait_send()

    def finish():
        if STOP < 1:
            early_drain()
        if STOP < 90:
            out_ref[...] = jnp.zeros_like(out_ref)
            loss_ref[...] = jnp.zeros_like(loss_ref)

    def early_drain():
        if STOP >= 0:
            gather_drain()

        def wsq(o, _):
            q_copy(o, dp).wait_send()
            return 0

        lax.fori_loop(1, DP, wsq, 0)

    def mid(it):
        stats_wait(it, NEAR)
        def near(h, _):
            numer(it, h, NEAR)
            return 0

        lax.fori_loop(0, CH, near, 0)
        stats_wait(it, FAR)
        def far(h, _):
            numer(it, h, FAR)
            pair_copy(it, h).start()
            return 0

        lax.fori_loop(0, CH, far, 0)
        for h in range(CH):
            pair_sum(it, h)

    if STOP == -2:
        for o in range(1, DP):
            q_copy(o, dp).start()
        lax.fori_loop(1, DP, q_wait, 0)
        for i in range(2, 5):
            loads[i].wait()
        return finish()
    if STOP == -1:
        for o in range(1, DP):
            q_copy(o, dp).start()
        early()
        return finish()
    if STOP == 0:
        gather(lambda d: None)
        return finish()
    softmax_first()
    owner_combine(0)
    early_drain()
    if STOP == 1:
        stats_wait(0, NEAR)
        stats_wait(0, FAR)
        stats_drain(0)
        return finish()
    query_post()
    if STOP == 2:
        stats_wait(0, NEAR)
        stats_wait(0, FAR)
        stats_drain(0)
        query_finish()
        return finish()
    mid(0)
    for h in range(CH):
        newc = update(0, h)
        own[h] = newc
        C2[quarter(h, y), 0:D] = newc.astype(BF16)
        C2[quarter(h, y), D:W] = three(jnp.sum(newc * newc, axis=1, keepdims=True), RQ)
        rows_send(0, h)
    stats_drain(0)
    for h in range(CH):
        rows_pass(0, h)
    if STOP == 5:
        for h in range(CH):
            rows_wait(0, h)
        reduce_drain(0)
        query_finish()
        return finish()

    softmax_second()
    owner_combine(1)
    query_finish()
    if STOP == 6:
        stats_wait(1, NEAR)
        stats_wait(1, FAR)
        stats_drain(1)
        reduce_drain(0)
        return finish()
    mid(1)
    for h in range(CH):
        out_ref[quarter(h, y), :] = update(1, h).astype(BF16)
        rows_send(1, h)
    stats_drain(1)
    reduce_drain(0)
    for h in range(CH):
        rows_pass(1, h)
    for h in range(CH):
        rows_wait(1, h)
    reduce_drain(1)
    finish()


def on_device(passages, queries, init_centroids, pattern, positive_offset):
    vm = pl.BlockSpec(memory_space=pltpu.VMEM)
    anywhere = pl.BlockSpec(memory_space=pl.ANY)
    dma = pltpu.SemaphoreType.DMA
    centroids, loss = pl.pallas_call(
        kernel,
        out_shape=(jax.ShapeDtypeStruct((KL, D), BF16), jax.ShapeDtypeStruct((1, 4), F32)),
        in_specs=[anywhere] * 5,
        out_specs=(vm, vm),
        scratch_shapes=[
            pltpu.VMEM((NZ, NX, BLOCK, D), BF16),
            pltpu.VMEM((NZ, KL, NX * BLOCK), F32),
            pltpu.VMEM((NZ, QP, NX * BLOCK), F32),
            pltpu.VMEM((KL + QP, D), BF16),
            pltpu.VMEM((KL, W), BF16),
            pltpu.VMEM((KL, 128), F32),
            pltpu.VMEM((2, KL, W), F32),
            pltpu.VMEM((2, CH, RH, W), F32),
            pltpu.VMEM((2, CH, RH, W), BF16),
            pltpu.VMEM((2, CH, NY, RQ, W), BF16),
            pltpu.VMEM((2, CH, NY, RQ, W), F32),
            pltpu.VMEM((CH, RQ, D), F32),
            pltpu.VMEM((KL, D), F32),
            pltpu.VMEM((4, D), BF16),
            pltpu.VMEM((4, 1024), jnp.int32),
            pltpu.VMEM((DP, 128), jnp.int32),
            pltpu.VMEM((5, QP, 128), F32),
            pltpu.VMEM((CENT, 2, 128), F32),
            pltpu.VMEM((2, CENT, 2, 128), F32),
            pltpu.VMEM((2, CENT, 2, 128), F32),
            pltpu.VMEM((8, D), F32),
            pltpu.VMEM((DP, 8, D), F32),
            pltpu.VMEM((DP, 8, 128), F32),
            pltpu.VMEM((DP, 8, 128), F32),
            dma, dma((NZ + 1,)), dma, dma((NZ, 2)),
            dma((2,)), dma((NZ, 4)), dma((4,)), dma((4,)),
            dma((DP,)), dma((DP,)),
            dma((2,)), dma((2,)),
            dma((2,)), dma((2, 2)),
            dma((2, CH)), dma((2, CH)),
            dma((2, CH, NY)), dma((2, CH, NY)),
            dma((2, CH, NY)), dma((2, CH, NY)),
            dma((DP,)), dma((DP,)),
            dma((5,)),
        ],
        compiler_params=pltpu.CompilerParams(
            collective_id=0, has_side_effects=True, vmem_limit_bytes=56 * 1024 * 1024
        ),
    )(passages, queries, init_centroids, pattern.T, positive_offset.reshape(DP, 128))
    return centroids.astype(F32), loss.reshape(4)


def solution(mesh):
    placed = (P(("dp", "cent"), None), P(("dp", "cent"), None), P("cent", None), P(), P())
    return jax.shard_map(
        on_device,
        mesh=mesh,
        in_specs=placed,
        out_specs=(P("cent", None), P(("dp", "cent"))),
        check_vma=False,
    )
```

```python
import jax
import jax.numpy as jnp
from jax import lax
from jax.experimental import pallas as pl
from jax.experimental.pallas import tpu as pltpu
from jax.sharding import PartitionSpec as P

MESH = pl.DeviceIdType.MESH
BLOCK = 128
D = 768
HD = 384
NX, NZ, NY = 4, 8, 4
CENT = NX * NZ
DP = 2 * NY
KL = 256
QP = 64
W = D + 128
CH = 2
RC = KL // CH
RH = RC // 2
RQ = RH // NY
sharpness = 0.05
NEG = -1e30
RA = 80
RB = 128 - RA
FAR, NEAR = (0, 1, 2, 3), (4, 5, 6, 7)
F32 = jnp.float32
BF16 = jnp.bfloat16


def rcopy(src, dst, ss, rs, dev):
    return pltpu.make_async_remote_copy(
        src_ref=src, dst_ref=dst, send_sem=ss, recv_sem=rs, device_id=dev, device_id_type=MESH
    )


def three(v, rows):
    lane = lax.broadcasted_iota(jnp.int32, (rows, 128), 1)
    v = jnp.broadcast_to(v, (rows, 128))
    hi = v.astype(BF16).astype(F32)
    mid = (v - hi).astype(BF16).astype(F32)
    lo = v - hi - mid
    return jnp.where(lane == 0, hi, jnp.where(lane == 1, mid, jnp.where(lane == 2, lo, 0.0))).astype(BF16)


def kernel(
    p_ref, q_ref, c_ref, pat_ref, off_ref, out_ref, loss_ref,
    G, E, S, CQ, C2, NB, acc, rb1, nar, rb2n, own, cv, qv, patv, offv, patb, st_s, st_r, rs_r,
    qs, qr, qp_s, qp_r,
    az_ss, az_rs, bz_ss, bz_rs, ax_ss, ax_rs, bx_ss, bx_rs, q_ss, q_rs, st_ss, st_rs, rs_ss, rs_rs,
    n1_ss, n1_rs, n2_ss, n2_rs, c_ss, c_rs, qp_ss, qp_rs, loc,
):
    dp = lax.axis_index("dp")
    me = lax.axis_index("cent")
    x, z = me // NZ, me % NZ
    y, core = dp // 2, dp % 2
    sib = (dp + 1 - 2 * core, me)
    z4 = (z + NZ // 2) % NZ

    def cdev(xx, zz):
        return (dp, xx * NZ + zz)

    loads = [
        pltpu.make_async_copy(src, dst, loc.at[i])
        for i, (src, dst) in enumerate(
            [(p_ref, G.at[z, x]), (q_ref, qv), (c_ref, cv), (pat_ref, patv), (off_ref, offv)]
        )
    ]
    for cp in loads:
        cp.start()

    barrier = pltpu.get_barrier_semaphore()
    for dev in (
        cdev(x, (z + 1) % NZ), cdev(x, (z + NZ - 1) % NZ),
        cdev((x + 1) % NX, z), cdev((x + 2) % NX, z), cdev((x + 3) % NX, z),
    ):
        pl.semaphore_signal(barrier, inc=1, device_id=dev, device_id_type=MESH)
    for o in range(1, DP):
        pl.semaphore_signal(barrier, inc=1, device_id=((dp + o) % DP, me), device_id_type=MESH)
    loads[1].wait()
    qs[...] = jnp.zeros_like(qs)
    qs[0:4, :] = qv[...].astype(F32)
    qr[dp] = qs[...]
    loads[0].wait()
    pl.semaphore_wait(barrier, 5 + DP - 1)

    def q_copy(o, src):
        return rcopy(qs, qr.at[src], q_ss.at[o], q_rs.at[src], ((dp + o) % DP, me))

    def zdev(step):
        return (dp, x * NZ + (z + NZ + step) % NZ)

    def xdev(step):
        return (dp, ((x + NX + step) % NX) * NZ + z)

    STEP = (1, -1)

    def a_z(zs, side, part=None):
        lo, n = (0, D) if part is None else (part * HD, HD)
        ref = G.at[zs, x, pl.ds(0, RA), pl.ds(lo, n)]
        return rcopy(ref, ref, az_ss, az_rs.at[zs if part != 1 else NZ], zdev(STEP[side]))

    def b_z(zs, side, part):
        ref = G.at[zs, pl.ds(part * (NX // 2), NX // 2), pl.ds(RA, RB)]
        return rcopy(ref, ref, bz_ss, bz_rs.at[zs, part], zdev(STEP[side]))

    def a_x(zs, xs, side):
        ref = G.at[zs, xs, pl.ds(0, RA)]
        return rcopy(ref, ref, ax_ss.at[0], ax_rs.at[zs, side], xdev(STEP[side]))

    def a_x2(zs, xs, side):
        ref = G.at[zs, xs, pl.ds(0, RA), pl.ds(side * HD, HD)]
        return rcopy(ref, ref, ax_ss.at[1], ax_rs.at[zs, 2 + side], xdev(STEP[side]))

    def b_x(xs, i):
        ref = G.at[z, xs, pl.ds(RA, RB)]
        return rcopy(ref, ref, bx_ss.at[i], bx_rs.at[i], xdev(i))

    def xfrom(side, n=1):
        return (x + NX - n * STEP[side]) % NX

    def zfrom(side, n):
        return (z + NZ - n * STEP[side]) % NZ

    def send_ax(zs):
        for side in range(2):
            a_x(zs, x, side).start()

    def hop_ax(zs):
        for side in range(2):
            a_x(zs, xfrom(side), side).wait_recv()
            a_x2(zs, xfrom(side), side).start()

    def end_ax(zs):
        for side in range(2):
            a_x2(zs, xfrom(side, 2), side).wait_recv()

    def take_a(d):
        for side in range(2):
            zs = zfrom(side, d)
            if d < 4:
                a_z(zs, side).wait_recv()
                a_z(zs, side, None if d < 3 else side).start()
                send_ax(zs)
            else:
                a_z(zs, side, side).wait_recv()
        if d == 4:
            send_ax(zfrom(0, 4))

    def take_b(d, part):
        for side in range(2):
            zs = zfrom(side, d)
            if d < 4:
                b_z(zs, side, part).wait_recv()
                if d < 3 or part == side:
                    b_z(zs, side, part).start()
            elif part == side:
                b_z(zs, side, part).wait_recv()

    def hop(d):
        for side in range(2 if 0 < d < 4 else 1):
            hop_ax(zfrom(side, d))

    def end(d):
        for side in range(2 if 0 < d < 4 else 1):
            end_ax(zfrom(side, d))

    def gather(compute):
        for side in range(2):
            a_z(z, side).start()
        for i in (2, 1, 3):
            b_x(x, i).start()
        send_ax(z)
        for o in range(1, DP):
            q_copy(o, dp).start()
        take_a(1)
        for i in (1, 3, 2):
            b_x((x + NX - i) % NX, i).wait_recv()
        for part in range(2):
            for side in range(2):
                b_z(z, side, part).start()
        take_a(2)
        hop(0)
        early()
        take_b(1, 0)
        take_b(1, 1)
        hop(1)
        hop(2)
        take_a(3)
        take_b(2, 0)
        take_b(2, 1)
        take_a(4)
        take_b(3, 0)
        end(1)
        hop(3)
        end(0)
        compute(0)
        end(2)
        compute(1)
        take_b(3, 1)
        hop(4)
        compute(2)
        end(3)
        compute(3)
        take_b(4, 0)
        take_b(4, 1)
        end(4)
        compute(4)

    def gather_drain():
        for i in range(1, NX):
            b_x(x, i).wait_send()

        def wait_all(ref, ss):
            rcopy(ref, ref, ss, bx_rs.at[0], sib).wait_send()

        flat = G.at[:, :, pl.ds(0, RA)]
        wait_all(flat.at[0, pl.ds(0, 1)], az_ss)
        wait_all(flat.at[pl.ds(0, 3), pl.ds(0, 2)], az_ss)
        wait_all(G.at[pl.ds(0, 7), :, pl.ds(RA, RB)], bz_ss)
        wait_all(flat.at[pl.ds(0, 4)], ax_ss.at[0])
        wait_all(flat.at[pl.ds(0, 2)], ax_ss.at[1])

    def q_wait(o, _):
        q_copy(o, (dp + DP - o) % DP).wait_recv()
        return 0

    def early():
        for i in range(2, 5):
            loads[i].wait()
        c0 = cv[...]
        CQ[0:KL, :] = c0.astype(BF16)
        NB[...] = jnp.broadcast_to(jnp.sum(c0 * c0, axis=1, keepdims=True), (KL, 128))
        lane = lax.broadcasted_iota(jnp.int32, (8, BLOCK), 1)
        sub = lax.broadcasted_iota(jnp.int32, (8, BLOCK), 0)
        pick = (lane == me * 4 + sub) & (sub < 4)
        for j in range(DP):
            for i in range(5):
                row = patv[i:i + 1, j * BLOCK:(j + 1) * BLOCK] if i < 4 else offv[j:j + 1, :]
                vals = jnp.where(pick, jnp.broadcast_to(row.astype(F32), (8, BLOCK)), 0.0)
                patb[i, 8 * j:8 * j + 8, :] = jnp.broadcast_to(jnp.sum(vals, axis=1, keepdims=True), (8, BLOCK))
        for o in range(1, DP):
            q_wait(o, 0)
        CQ[KL:KL + QP, :] = qr[...].reshape(QP, D).astype(BF16)

    def column(k):
        d = (k + 1) // 2
        sgn = 1 - 2 * (k % 2)
        return (z + NZ + sgn * d) % NZ

    def st_copy(it, xc, zc, xs, zs):
        return rcopy(
            st_s.at[zc * NX + xc], st_r.at[it, zs * NX + xs], st_ss.at[it], st_rs.at[it],
            cdev(xc, (zc + NZ // 2) % NZ),
        )

    def dot_nt(lhs, rhs):
        return lax.dot_general(lhs, rhs, (((1,), (1,)), ((), ())), preferred_element_type=F32)

    def ship(it, zc, mine):
        if mine:
            st_r[it, z * NX + x] = st_s[z4 * NX + x]
            for i in range(1, NX):
                st_copy(it, (x + i) % NX, z4, x, z).start()
        else:
            for xc in range(NX):
                st_copy(it, xc, zc, x, z).start()

    def columns(it, zcs):
        for zc in zcs:
            lhs = CQ[...] if it == 0 else C2[:, 0:D]
            dots = dot_nt(lhs, G[zc].reshape(NX * BLOCK, D))
            nb = NB[...]
            for xc in range(NX):
                a = xc * BLOCK
                ll = sharpness * (2.0 * dots[0:KL, a:a + BLOCK] - nb)
                m = jnp.max(ll, axis=0, keepdims=True)
                e = jnp.exp(ll - m)
                E[zc, :, a:a + BLOCK] = e
                st_s[zc * NX + xc, 0:1, :] = m
                st_s[zc * NX + xc, 1:2, :] = jnp.sum(e, axis=0, keepdims=True)
            if it == 0:
                S[zc] = dots[KL:KL + QP, :] * sharpness

    def softmax_first():
        def compute(d):
            zcs = [zfrom(side, d) for side in range(2 if 0 < d < 4 else 1)]
            columns(0, zcs)
            for zc in zcs:
                ship(0, zc, d == 4)

        gather(compute)

    def softmax_second():
        for h in range(CH):
            rows_wait(0, h)
            rows = slice(h * RC, (h + 1) * RC)
            NB[rows, :] = jnp.broadcast_to(
                jnp.sum(C2[rows, D:W].astype(F32), axis=1, keepdims=True), (RC, 128)
            )
        for grp in (FAR, NEAR):
            columns(1, [column(k) for k in grp])
            for k in grp:
                ship(1, column(k), k == 7)

    def rs_copy(it, dx, dz):
        ref = rs_r.at[it, z4 * NX + x]
        far = 1 if dz in (3, 4, 5, 6) else 0
        return rcopy(ref, ref, rs_ss.at[it], rs_rs.at[it, far], cdev((x + dx) % NX, (z + dz) % NZ))

    def all_of(ref, n, ss, rs):
        some = ref.at[pl.ds(0, n)]
        return rcopy(some, some, ss, rs, sib)

    def owner_combine(it):
        all_of(st_r.at[it], CENT - 1, st_ss.at[it], st_rs.at[it]).wait_recv()
        m = st_r[it, :, 0:1, :]
        s = st_r[it, :, 1:2, :]
        top = jnp.max(m, axis=0)
        tot = jnp.sum(s * jnp.exp(m - top[None]), axis=0)
        rs_r[it, z4 * NX + x, 0:1, :] = top
        rs_r[it, z4 * NX + x, 1:2, :] = 1.0 / tot
        for dz in (4, 3, 5, 6, 2, 1, 7, 0):
            for dx in (2, 1, 3, 0):
                if dz or dx:
                    rs_copy(it, dx, dz).start()

    def query_post():
        pats = [patb[i] for i in range(4)]
        off = patb[4]
        lane = lax.broadcasted_iota(jnp.int32, (QP, BLOCK), 1)
        lanef = lane.astype(F32)

        def allow_of(b):
            return (pats[0] == b) | (pats[1] == b) | (pats[2] == b) | (pats[3] == b)

        def p1(zc, mx):
            for xc in range(NX):
                b = (dp * CENT + xc * NZ + zc).astype(F32)
                sv = S[zc, :, xc * BLOCK:(xc + 1) * BLOCK]
                mx = jnp.maximum(mx, jnp.where(allow_of(b), sv, NEG))
            return mx

        mx = lax.fori_loop(0, NZ, p1, jnp.full((QP, BLOCK), NEG, F32))
        mrow = jnp.max(mx, axis=1, keepdims=True)
        mb = jnp.broadcast_to(mrow, (QP, BLOCK))

        def p2(zc, carry):
            tot, pos = carry
            for xc in range(NX):
                b = (dp * CENT + xc * NZ + zc).astype(F32)
                sv = S[zc, :, xc * BLOCK:(xc + 1) * BLOCK]
                tot = tot + jnp.where(allow_of(b), jnp.exp(sv - mb), 0.0)
                pos = pos + jnp.where((pats[0] == b) & (lanef == off), sv, 0.0)
            return tot, pos

        zero = jnp.zeros((QP, BLOCK), F32)
        tot, pos = lax.fori_loop(0, NZ, p2, (zero, zero))
        trow = jnp.broadcast_to(jnp.sum(tot, axis=1, keepdims=True), (QP, BLOCK))
        prow = jnp.broadcast_to(jnp.sum(pos, axis=1, keepdims=True), (QP, BLOCK))
        packed = jnp.where(lane == 0, mb, jnp.where(lane == 1, trow, prow))
        qp_s[...] = packed.reshape(DP, 8, BLOCK)
        qp_r[dp] = qp_s[dp]

        def snd(o, _):
            qp_copy(o, (dp + o) % DP, dp).start()
            return 0

        lax.fori_loop(1, DP, snd, 0)

    def qp_copy(o, dst, src):
        return rcopy(qp_s.at[dst], qp_r.at[src], qp_ss.at[o], qp_rs.at[src], (dst, me))

    def query_finish():
        def w(o, _):
            qp_copy(o, (dp + o) % DP, (dp + o) % DP).wait_recv()
            return 0

        lax.fori_loop(1, DP, w, 0)
        m = qp_r[:, :, 0:1]
        t = qp_r[:, :, 1:2]
        p = qp_r[:, :, 2:3]
        top = jnp.max(m, axis=0)
        tot = jnp.sum(t * jnp.exp(m - top[None]), axis=0)
        ps = jnp.sum(p, axis=0)
        loss = jnp.broadcast_to(jnp.log(tot) + top - ps, (8, BLOCK))
        lane = lax.broadcasted_iota(jnp.int32, (8, BLOCK), 1)
        sub = lax.broadcasted_iota(jnp.int32, (8, BLOCK), 0)
        loss_ref[...] = jnp.sum(jnp.where(lane == sub, loss, 0.0), axis=0, keepdims=True)[:, 0:4]

        def ws(o, _):
            qp_copy(o, (dp + o) % DP, dp).wait_send()
            return 0

        lax.fori_loop(1, DP, ws, 0)

    def stats_wait(it, grp):
        n, far = (16, 1) if grp is FAR else (15, 0)
        all_of(rs_r.at[it], n, rs_ss.at[it], rs_rs.at[it, far]).wait_recv()

    def stats_drain(it):
        all_of(st_r.at[it], CENT - 1, st_ss.at[it], st_rs.at[it]).wait_send()
        all_of(rs_r.at[it], CENT - 1, rs_ss.at[it], rs_rs.at[it, 0]).wait_send()

    def numer(it, h, grp):
        rows = pl.ds(pl.multiple_of(h * RC, RC), RC)
        cnt = jnp.zeros((RC, BLOCK), F32)
        tot = jnp.zeros((RC, D), F32)
        for k in grp:
            zc = column(k)
            parts = []
            for xc in range(NX):
                a = xc * BLOCK
                g = jnp.exp(st_s[zc * NX + xc, 0:1, :] - rs_r[it, zc * NX + xc, 0:1, :]) * rs_r[it, zc * NX + xc, 1:2, :]
                r = E[zc, rows, a:a + BLOCK] * g
                cnt = cnt + r
                parts.append(r.astype(BF16))
            tot = tot + jnp.dot(
                jnp.concatenate(parts, axis=1), G[zc].reshape(NX * BLOCK, D), preferred_element_type=F32
            )
        if grp is NEAR:
            acc[it, rows, 0:D] = tot
            acc[it, rows, D:W] = cnt
        else:
            acc[it, rows, 0:D] += tot
            acc[it, rows, D:W] += cnt

    mine_at = [pl.multiple_of(h * RC + core * RH, RH) for h in range(CH)]
    theirs_at = [pl.multiple_of(h * RC + RH - core * RH, RH) for h in range(CH)]

    def pair_copy(it, h):
        return rcopy(acc.at[it, pl.ds(pl.multiple_of(h * RC + RH - core * RH, RH), RH)], rb1.at[it, h], n1_ss.at[it, h], n1_rs.at[it, h], sib)

    def quarter(h, yy):
        return pl.ds(pl.multiple_of(h * RC + core * RH + yy * RQ, RQ), RQ)

    def y_copy(it, h, i):
        yp = (y + i) % NY
        sem = (n2_ss.at[it, h], n2_rs.at[it, h])
        src = nar.at[it, h, pl.ds(pl.multiple_of(yp * RQ, RQ), RQ)]
        return rcopy(src, rb2n.at[it, h, i], *sem, (yp * 2 + core, me))

    def pair_sum(it, h):
        pair_copy(it, h).wait_recv()
        tot = acc[it, pl.ds(mine_at[h], RH), :] + rb1[it, h]
        acc[it, pl.ds(mine_at[h], RH), :] = tot
        nar[it, h, :, 0:D] = tot[:, 0:D].astype(BF16)
        nar[it, h, :, D:W] = three(jnp.sum(tot[:, D:W], axis=1, keepdims=True), RH)
        for i in (2, 1, 3):
            y_copy(it, h, i).start()

    def update(it, h):
        tot = acc[it, quarter(h, y), :]
        got = rb2n.at[it, h, pl.ds(1, NY - 1)]
        rcopy(got, got, n2_ss.at[it, h], n2_rs.at[it, h], sib).wait_recv()
        for i in (1, 2, 3):
            tot = tot + rb2n[it, h, i].astype(F32)
        counts = jnp.sum(tot[:, D:W], axis=1, keepdims=True)
        cold = cv[quarter(h, y), :] if it == 0 else own[h]
        return (tot[:, 0:D] + cold) / (counts + 1.0)

    def row_copy(k, h, i):
        arr = C2 if k == 0 else out_ref
        ref = arr.at[quarter(h, y)]
        return rcopy(ref, ref, c_ss.at[k, h, 1], c_rs.at[k, h, 1], (((y + i) % NY) * 2 + core, me))

    def half_copy(k, h):
        arr = C2 if k == 0 else out_ref
        ref = arr.at[pl.ds(mine_at[h], RH)]
        return rcopy(ref, ref, c_ss.at[k, h, 0], c_rs.at[k, h, 0], sib)

    def rows_send(k, h):
        for i in (2, 1, 3):
            row_copy(k, h, i).start()

    def rows_pass(k, h):
        arr = C2 if k == 0 else out_ref
        got = arr.at[pl.ds(0, 3 * RQ)]
        rcopy(got, got, c_ss.at[k, h, 1], c_rs.at[k, h, 1], sib).wait_recv()
        half_copy(k, h).start()

    def rows_wait(k, h):
        half_copy(k, h).wait_recv()

    def reduce_drain(it):
        for h in range(CH):
            pair_copy(it, h).wait_send()
            sent = rb2n.at[it, h, pl.ds(1, NY - 1)]
            rcopy(sent, sent, n2_ss.at[it, h], n2_rs.at[it, h], sib).wait_send()
            arr = C2 if it == 0 else out_ref
            sent = arr.at[pl.ds(0, 3 * RQ)]
            rcopy(sent, sent, c_ss.at[it, h, 1], c_rs.at[it, h, 1], sib).wait_send()
            half_copy(it, h).wait_send()

    def early_drain():
        gather_drain()

        def wsq(o, _):
            q_copy(o, dp).wait_send()
            return 0

        lax.fori_loop(1, DP, wsq, 0)

    def mid(it):
        stats_wait(it, NEAR)
        def near(h, _):
            numer(it, h, NEAR)
            return 0

        lax.fori_loop(0, CH, near, 0)
        stats_wait(it, FAR)
        def far(h, _):
            numer(it, h, FAR)
            pair_copy(it, h).start()
            return 0

        lax.fori_loop(0, CH, far, 0)
        for h in range(CH):
            pair_sum(it, h)

    softmax_first()
    owner_combine(0)
    early_drain()
    query_post()
    mid(0)
    for h in range(CH):
        newc = update(0, h)
        own[h] = newc
        C2[quarter(h, y), 0:D] = newc.astype(BF16)
        C2[quarter(h, y), D:W] = three(jnp.sum(newc * newc, axis=1, keepdims=True), RQ)
        rows_send(0, h)
    stats_drain(0)
    for h in range(CH):
        rows_pass(0, h)

    softmax_second()
    owner_combine(1)
    query_finish()
    mid(1)
    for h in range(CH):
        out_ref[quarter(h, y), :] = update(1, h).astype(BF16)
        rows_send(1, h)
    stats_drain(1)
    reduce_drain(0)
    for h in range(CH):
        rows_pass(1, h)
    for h in range(CH):
        rows_wait(1, h)
    reduce_drain(1)


def on_device(passages, queries, init_centroids, pattern, positive_offset):
    vm = pl.BlockSpec(memory_space=pltpu.VMEM)
    anywhere = pl.BlockSpec(memory_space=pl.ANY)
    dma = pltpu.SemaphoreType.DMA
    centroids, loss = pl.pallas_call(
        kernel,
        out_shape=(jax.ShapeDtypeStruct((KL, D), BF16), jax.ShapeDtypeStruct((1, 4), F32)),
        in_specs=[anywhere] * 5,
        out_specs=(vm, vm),
        scratch_shapes=[
            pltpu.VMEM((NZ, NX, BLOCK, D), BF16),
            pltpu.VMEM((NZ, KL, NX * BLOCK), F32),
            pltpu.VMEM((NZ, QP, NX * BLOCK), F32),
            pltpu.VMEM((KL + QP, D), BF16),
            pltpu.VMEM((KL, W), BF16),
            pltpu.VMEM((KL, 128), F32),
            pltpu.VMEM((2, KL, W), F32),
            pltpu.VMEM((2, CH, RH, W), F32),
            pltpu.VMEM((2, CH, RH, W), BF16),
            pltpu.VMEM((2, CH, NY, RQ, W), BF16),
            pltpu.VMEM((CH, RQ, D), F32),
            pltpu.VMEM((KL, D), F32),
            pltpu.VMEM((4, D), BF16),
            pltpu.VMEM((4, 1024), jnp.int32),
            pltpu.VMEM((DP, 128), jnp.int32),
            pltpu.VMEM((5, QP, 128), F32),
            pltpu.VMEM((CENT, 2, 128), F32),
            pltpu.VMEM((2, CENT, 2, 128), F32),
            pltpu.VMEM((2, CENT, 2, 128), F32),
            pltpu.VMEM((8, D), F32),
            pltpu.VMEM((DP, 8, D), F32),
            pltpu.VMEM((DP, 8, 128), F32),
            pltpu.VMEM((DP, 8, 128), F32),
            dma, dma((NZ + 1,)), dma, dma((NZ, 2)),
            dma((2,)), dma((NZ, 4)), dma((4,)), dma((4,)),
            dma((DP,)), dma((DP,)),
            dma((2,)), dma((2,)),
            dma((2,)), dma((2, 2)),
            dma((2, CH)), dma((2, CH)),
            dma((2, CH)), dma((2, CH)),
            dma((2, CH, 2)), dma((2, CH, 2)),
            dma((DP,)), dma((DP,)),
            dma((5,)),
        ],
        compiler_params=pltpu.CompilerParams(
            collective_id=0, has_side_effects=True, vmem_limit_bytes=56 * 1024 * 1024
        ),
    )(passages, queries, init_centroids, pattern.T, positive_offset.reshape(DP, 128))
    return centroids.astype(F32), loss.reshape(4)


def solution(mesh):
    placed = (P(("dp", "cent"), None), P(("dp", "cent"), None), P("cent", None), P(), P())
    return jax.shard_map(
        on_device,
        mesh=mesh,
        in_specs=placed,
        out_specs=(P("cent", None), P(("dp", "cent"))),
        check_vma=False,
    )
```

```python
import jax
import jax.numpy as jnp
from jax import lax
from jax.experimental import pallas as pl
from jax.experimental.pallas import tpu as pltpu
from jax.sharding import PartitionSpec as P

MESH = pl.DeviceIdType.MESH
BLOCK = 128
D = 768
HD = 384
NX, NZ, NY = 4, 8, 4
CENT = NX * NZ
DP = 2 * NY
KL = 256
QP = 64
W = D + 128
CH = 2
RC = KL // CH
RH = RC // 2
RQ = RH // NY
sharpness = 0.05
NEG = -1e30
RA = 80
RB = 128 - RA
FAR, NEAR = (0, 1, 2, 3), (4, 5, 6, 7)
F32 = jnp.float32
BF16 = jnp.bfloat16


def rcopy(src, dst, ss, rs, dev):
    return pltpu.make_async_remote_copy(
        src_ref=src, dst_ref=dst, send_sem=ss, recv_sem=rs, device_id=dev, device_id_type=MESH
    )


def three(v, rows):
    lane = lax.broadcasted_iota(jnp.int32, (rows, 128), 1)
    v = jnp.broadcast_to(v, (rows, 128))
    hi = v.astype(BF16).astype(F32)
    mid = (v - hi).astype(BF16).astype(F32)
    lo = v - hi - mid
    return jnp.where(lane == 0, hi, jnp.where(lane == 1, mid, jnp.where(lane == 2, lo, 0.0))).astype(BF16)


def kernel(
    p_ref, q_ref, c_ref, pat_ref, off_ref, out_ref, loss_ref,
    G, E, S, CQ, C2, NB, acc, rb1, nar, rb2n, own, cv, qv, patv, offv, patb, st_s, st_r, rs_r,
    qs, qr, qp_s, qp_r,
    az_ss, az_rs, bz_ss, bz_rs, ax_ss, ax_rs, bx_ss, bx_rs, q_ss, q_rs, st_ss, st_rs, rs_ss, rs_rs,
    n1_ss, n1_rs, n2_ss, n2_rs, c_ss, c_rs, qp_ss, qp_rs, loc,
):
    dp = lax.axis_index("dp")
    me = lax.axis_index("cent")
    x, z = me // NZ, me % NZ
    y, core = dp // 2, dp % 2
    sib = (dp + 1 - 2 * core, me)
    z4 = (z + NZ // 2) % NZ

    def cdev(xx, zz):
        return (dp, xx * NZ + zz)

    loads = [
        pltpu.make_async_copy(src, dst, loc.at[i])
        for i, (src, dst) in enumerate(
            [(p_ref, G.at[z, x]), (q_ref, qv), (c_ref, cv), (pat_ref, patv), (off_ref, offv)]
        )
    ]
    for cp in loads:
        cp.start()

    barrier = pltpu.get_barrier_semaphore()
    for dev in (
        cdev(x, (z + 1) % NZ), cdev(x, (z + NZ - 1) % NZ),
        cdev((x + 1) % NX, z), cdev((x + 2) % NX, z), cdev((x + 3) % NX, z),
    ):
        pl.semaphore_signal(barrier, inc=1, device_id=dev, device_id_type=MESH)
    for o in range(1, DP):
        pl.semaphore_signal(barrier, inc=1, device_id=((dp + o) % DP, me), device_id_type=MESH)
    loads[1].wait()
    qs[...] = jnp.zeros_like(qs)
    qs[0:4, :] = qv[...].astype(F32)
    qr[dp] = qs[...]
    loads[0].wait()
    pl.semaphore_wait(barrier, 5 + DP - 1)

    def q_copy(o, src):
        return rcopy(qs, qr.at[src], q_ss.at[o], q_rs.at[src], ((dp + o) % DP, me))

    def zdev(step):
        return (dp, x * NZ + (z + NZ + step) % NZ)

    def xdev(step):
        return (dp, ((x + NX + step) % NX) * NZ + z)

    STEP = (1, -1)

    def a_z(zs, side, part=None):
        lo, n = (0, D) if part is None else (part * HD, HD)
        ref = G.at[zs, x, pl.ds(0, RA), pl.ds(lo, n)]
        return rcopy(ref, ref, az_ss, az_rs.at[zs if part != 1 else NZ], zdev(STEP[side]))

    def b_z(zs, side, part):
        ref = G.at[zs, pl.ds(part * (NX // 2), NX // 2), pl.ds(RA, RB)]
        return rcopy(ref, ref, bz_ss, bz_rs.at[zs, part], zdev(STEP[side]))

    def a_x(zs, xs, side):
        ref = G.at[zs, xs, pl.ds(0, RA)]
        return rcopy(ref, ref, ax_ss.at[0], ax_rs.at[zs, side], xdev(STEP[side]))

    def a_x2(zs, xs, side):
        ref = G.at[zs, xs, pl.ds(0, RA), pl.ds(side * HD, HD)]
        return rcopy(ref, ref, ax_ss.at[1], ax_rs.at[zs, 2 + side], xdev(STEP[side]))

    def b_x(xs, i):
        ref = G.at[z, xs, pl.ds(RA, RB)]
        return rcopy(ref, ref, bx_ss.at[i], bx_rs.at[i], xdev(i))

    def xfrom(side, n=1):
        return (x + NX - n * STEP[side]) % NX

    def zfrom(side, n):
        return (z + NZ - n * STEP[side]) % NZ

    def send_ax(zs):
        for side in range(2):
            a_x(zs, x, side).start()

    def hop_ax(zs):
        for side in range(2):
            a_x(zs, xfrom(side), side).wait_recv()
            a_x2(zs, xfrom(side), side).start()

    def end_ax(zs):
        for side in range(2):
            a_x2(zs, xfrom(side, 2), side).wait_recv()

    def take_a(d):
        for side in range(2):
            zs = zfrom(side, d)
            if d < 4:
                a_z(zs, side).wait_recv()
                a_z(zs, side, None if d < 3 else side).start()
                send_ax(zs)
            else:
                a_z(zs, side, side).wait_recv()
        if d == 4:
            send_ax(zfrom(0, 4))

    def take_b(d, part):
        for side in range(2):
            zs = zfrom(side, d)
            if d < 4:
                b_z(zs, side, part).wait_recv()
                if d < 3 or part == side:
                    b_z(zs, side, part).start()
            elif part == side:
                b_z(zs, side, part).wait_recv()

    def hop(d):
        for side in range(2 if 0 < d < 4 else 1):
            hop_ax(zfrom(side, d))

    def end(d):
        for side in range(2 if 0 < d < 4 else 1):
            end_ax(zfrom(side, d))

    def gather(compute):
        for side in range(2):
            a_z(z, side).start()
        for i in (2, 1, 3):
            b_x(x, i).start()
        send_ax(z)
        for o in range(1, DP):
            q_copy(o, dp).start()
        take_a(1)
        for i in (1, 3, 2):
            b_x((x + NX - i) % NX, i).wait_recv()
        for part in range(2):
            for side in range(2):
                b_z(z, side, part).start()
        take_a(2)
        hop(0)
        early()
        take_b(1, 0)
        take_b(1, 1)
        hop(1)
        hop(2)
        take_a(3)
        take_b(2, 0)
        take_b(2, 1)
        take_a(4)
        take_b(3, 0)
        end(1)
        hop(3)
        end(0)
        compute(0)
        end(2)
        compute(1)
        take_b(3, 1)
        hop(4)
        compute(2)
        end(3)
        compute(3)
        take_b(4, 0)
        take_b(4, 1)
        end(4)
        compute(4)

    def gather_drain():
        for i in range(1, NX):
            b_x(x, i).wait_send()

        def wait_all(ref, ss):
            rcopy(ref, ref, ss, bx_rs.at[0], sib).wait_send()

        flat = G.at[:, :, pl.ds(0, RA)]
        wait_all(flat.at[0, pl.ds(0, 1)], az_ss)
        wait_all(flat.at[pl.ds(0, 3), pl.ds(0, 2)], az_ss)
        wait_all(G.at[pl.ds(0, 7), :, pl.ds(RA, RB)], bz_ss)
        wait_all(flat.at[pl.ds(0, 4)], ax_ss.at[0])
        wait_all(flat.at[pl.ds(0, 2)], ax_ss.at[1])

    def q_wait(o, _):
        q_copy(o, (dp + DP - o) % DP).wait_recv()
        return 0

    def early():
        for i in range(2, 5):
            loads[i].wait()
        c0 = cv[...]
        CQ[0:KL, :] = c0.astype(BF16)
        NB[...] = jnp.broadcast_to(jnp.sum(c0 * c0, axis=1, keepdims=True), (KL, 128))
        lane = lax.broadcasted_iota(jnp.int32, (8, BLOCK), 1)
        sub = lax.broadcasted_iota(jnp.int32, (8, BLOCK), 0)
        pick = (lane == me * 4 + sub) & (sub < 4)
        for j in range(DP):
            for i in range(5):
                row = patv[i:i + 1, j * BLOCK:(j + 1) * BLOCK] if i < 4 else offv[j:j + 1, :]
                vals = jnp.where(pick, jnp.broadcast_to(row.astype(F32), (8, BLOCK)), 0.0)
                patb[i, 8 * j:8 * j + 8, :] = jnp.broadcast_to(jnp.sum(vals, axis=1, keepdims=True), (8, BLOCK))
        for o in range(1, DP):
            q_wait(o, 0)
        CQ[KL:KL + QP, :] = qr[...].reshape(QP, D).astype(BF16)

    def column(k):
        d = (k + 1) // 2
        sgn = 1 - 2 * (k % 2)
        return (z + NZ + sgn * d) % NZ

    def st_copy(it, xc, zc, xs, zs):
        return rcopy(
            st_s.at[zc * NX + xc], st_r.at[it, zs * NX + xs], st_ss.at[it], st_rs.at[it],
            cdev(xc, (zc + NZ // 2) % NZ),
        )

    def dot_nt(lhs, rhs):
        return lax.dot_general(lhs, rhs, (((1,), (1,)), ((), ())), preferred_element_type=F32)

    def ship(it, zc, mine):
        if mine:
            st_r[it, z * NX + x] = st_s[z4 * NX + x]
            for i in (2, 1, 3):
                st_copy(it, (x + i) % NX, z4, x, z).start()
        else:
            for i in (2, 1, 3, 0):
                st_copy(it, (x + i) % NX, zc, x, z).start()

    def columns(it, zcs):
        for zc in zcs:
            lhs = CQ[...] if it == 0 else C2[:, 0:D]
            dots = dot_nt(lhs, G[zc].reshape(NX * BLOCK, D))
            nb = NB[...]
            for xc in range(NX):
                a = xc * BLOCK
                ll = sharpness * (2.0 * dots[0:KL, a:a + BLOCK] - nb)
                m = jnp.max(ll, axis=0, keepdims=True)
                e = jnp.exp(ll - m)
                E[zc, :, a:a + BLOCK] = e
                st_s[zc * NX + xc, 0:1, :] = m
                st_s[zc * NX + xc, 1:2, :] = jnp.sum(e, axis=0, keepdims=True)
            if it == 0:
                S[zc] = dots[KL:KL + QP, :] * sharpness

    def softmax_first():
        def compute(d):
            zcs = [zfrom(side, d) for side in range(2 if 0 < d < 4 else 1)]
            columns(0, zcs)
            for zc in zcs:
                ship(0, zc, d == 4)

        gather(compute)

    def softmax_second():
        for h in range(CH):
            rows_wait(0, h)
            rows = slice(h * RC, (h + 1) * RC)
            NB[rows, :] = jnp.broadcast_to(
                jnp.sum(C2[rows, D:W].astype(F32), axis=1, keepdims=True), (RC, 128)
            )
        for grp in (FAR, NEAR):
            columns(1, [column(k) for k in grp])
            for k in grp:
                ship(1, column(k), k == 7)

    def rs_copy(it, dx, dz):
        ref = rs_r.at[it, z4 * NX + x]
        far = 1 if dz in (3, 4, 5, 6) else 0
        return rcopy(ref, ref, rs_ss.at[it], rs_rs.at[it, far], cdev((x + dx) % NX, (z + dz) % NZ))

    def all_of(ref, n, ss, rs):
        some = ref.at[pl.ds(0, n)]
        return rcopy(some, some, ss, rs, sib)

    def owner_combine(it):
        all_of(st_r.at[it], CENT - 1, st_ss.at[it], st_rs.at[it]).wait_recv()
        m = st_r[it, :, 0:1, :]
        s = st_r[it, :, 1:2, :]
        top = jnp.max(m, axis=0)
        tot = jnp.sum(s * jnp.exp(m - top[None]), axis=0)
        rs_r[it, z4 * NX + x, 0:1, :] = top
        rs_r[it, z4 * NX + x, 1:2, :] = 1.0 / tot
        for dz in (4, 3, 5, 6, 2, 1, 7, 0):
            for dx in (2, 1, 3, 0):
                if dz or dx:
                    rs_copy(it, dx, dz).start()

    def query_post():
        pats = [patb[i] for i in range(4)]
        off = patb[4]
        lane = lax.broadcasted_iota(jnp.int32, (QP, BLOCK), 1)
        lanef = lane.astype(F32)

        def allow_of(b):
            return (pats[0] == b) | (pats[1] == b) | (pats[2] == b) | (pats[3] == b)

        def p1(zc, mx):
            for xc in range(NX):
                b = (dp * CENT + xc * NZ + zc).astype(F32)
                sv = S[zc, :, xc * BLOCK:(xc + 1) * BLOCK]
                mx = jnp.maximum(mx, jnp.where(allow_of(b), sv, NEG))
            return mx

        mx = lax.fori_loop(0, NZ, p1, jnp.full((QP, BLOCK), NEG, F32))
        mrow = jnp.max(mx, axis=1, keepdims=True)
        mb = jnp.broadcast_to(mrow, (QP, BLOCK))

        def p2(zc, carry):
            tot, pos = carry
            for xc in range(NX):
                b = (dp * CENT + xc * NZ + zc).astype(F32)
                sv = S[zc, :, xc * BLOCK:(xc + 1) * BLOCK]
                tot = tot + jnp.where(allow_of(b), jnp.exp(sv - mb), 0.0)
                pos = pos + jnp.where((pats[0] == b) & (lanef == off), sv, 0.0)
            return tot, pos

        zero = jnp.zeros((QP, BLOCK), F32)
        tot, pos = lax.fori_loop(0, NZ, p2, (zero, zero))
        trow = jnp.broadcast_to(jnp.sum(tot, axis=1, keepdims=True), (QP, BLOCK))
        prow = jnp.broadcast_to(jnp.sum(pos, axis=1, keepdims=True), (QP, BLOCK))
        packed = jnp.where(lane == 0, mb, jnp.where(lane == 1, trow, prow))
        qp_s[...] = packed.reshape(DP, 8, BLOCK)
        qp_r[dp] = qp_s[dp]

        def snd(o, _):
            qp_copy(o, (dp + o) % DP, dp).start()
            return 0

        lax.fori_loop(1, DP, snd, 0)

    def qp_copy(o, dst, src):
        return rcopy(qp_s.at[dst], qp_r.at[src], qp_ss.at[o], qp_rs.at[src], (dst, me))

    def query_finish():
        def w(o, _):
            qp_copy(o, (dp + o) % DP, (dp + o) % DP).wait_recv()
            return 0

        lax.fori_loop(1, DP, w, 0)
        m = qp_r[:, :, 0:1]
        t = qp_r[:, :, 1:2]
        p = qp_r[:, :, 2:3]
        top = jnp.max(m, axis=0)
        tot = jnp.sum(t * jnp.exp(m - top[None]), axis=0)
        ps = jnp.sum(p, axis=0)
        loss = jnp.broadcast_to(jnp.log(tot) + top - ps, (8, BLOCK))
        lane = lax.broadcasted_iota(jnp.int32, (8, BLOCK), 1)
        sub = lax.broadcasted_iota(jnp.int32, (8, BLOCK), 0)
        loss_ref[...] = jnp.sum(jnp.where(lane == sub, loss, 0.0), axis=0, keepdims=True)[:, 0:4]

        def ws(o, _):
            qp_copy(o, (dp + o) % DP, dp).wait_send()
            return 0

        lax.fori_loop(1, DP, ws, 0)

    def stats_wait(it, grp):
        n, far = (16, 1) if grp is FAR else (15, 0)
        all_of(rs_r.at[it], n, rs_ss.at[it], rs_rs.at[it, far]).wait_recv()

    def stats_drain(it):
        all_of(st_r.at[it], CENT - 1, st_ss.at[it], st_rs.at[it]).wait_send()
        all_of(rs_r.at[it], CENT - 1, rs_ss.at[it], rs_rs.at[it, 0]).wait_send()

    def numer(it, h, grp):
        rows = pl.ds(pl.multiple_of(h * RC, RC), RC)
        cnt = jnp.zeros((RC, BLOCK), F32)
        tot = jnp.zeros((RC, D), F32)
        for k in grp:
            zc = column(k)
            parts = []
            for xc in range(NX):
                a = xc * BLOCK
                g = jnp.exp(st_s[zc * NX + xc, 0:1, :] - rs_r[it, zc * NX + xc, 0:1, :]) * rs_r[it, zc * NX + xc, 1:2, :]
                r = E[zc, rows, a:a + BLOCK] * g
                cnt = cnt + r
                parts.append(r.astype(BF16))
            tot = tot + jnp.dot(
                jnp.concatenate(parts, axis=1), G[zc].reshape(NX * BLOCK, D), preferred_element_type=F32
            )
        if grp is NEAR:
            acc[it, rows, 0:D] = tot
            acc[it, rows, D:W] = cnt
        else:
            acc[it, rows, 0:D] += tot
            acc[it, rows, D:W] += cnt

    mine_at = [pl.multiple_of(h * RC + core * RH, RH) for h in range(CH)]
    theirs_at = [pl.multiple_of(h * RC + RH - core * RH, RH) for h in range(CH)]

    def pair_copy(it, h):
        return rcopy(acc.at[it, pl.ds(pl.multiple_of(h * RC + RH - core * RH, RH), RH)], rb1.at[it, h], n1_ss.at[it, h], n1_rs.at[it, h], sib)

    def quarter(h, yy):
        return pl.ds(pl.multiple_of(h * RC + core * RH + yy * RQ, RQ), RQ)

    def y_copy(it, h, i):
        yp = (y + i) % NY
        sem = (n2_ss.at[it, h], n2_rs.at[it, h])
        src = nar.at[it, h, pl.ds(pl.multiple_of(yp * RQ, RQ), RQ)]
        return rcopy(src, rb2n.at[it, h, i], *sem, (yp * 2 + core, me))

    def pair_sum(it, h):
        pair_copy(it, h).wait_recv()
        tot = acc[it, pl.ds(mine_at[h], RH), :] + rb1[it, h]
        acc[it, pl.ds(mine_at[h], RH), :] = tot
        nar[it, h, :, 0:D] = tot[:, 0:D].astype(BF16)
        nar[it, h, :, D:W] = three(jnp.sum(tot[:, D:W], axis=1, keepdims=True), RH)
        for i in (2, 1, 3):
            y_copy(it, h, i).start()

    def update(it, h):
        tot = acc[it, quarter(h, y), :]
        got = rb2n.at[it, h, pl.ds(1, NY - 1)]
        rcopy(got, got, n2_ss.at[it, h], n2_rs.at[it, h], sib).wait_recv()
        for i in (1, 2, 3):
            tot = tot + rb2n[it, h, i].astype(F32)
        counts = jnp.sum(tot[:, D:W], axis=1, keepdims=True)
        cold = cv[quarter(h, y), :] if it == 0 else own[h]
        return (tot[:, 0:D] + cold) / (counts + 1.0)

    def row_copy(k, h, i):
        arr = C2 if k == 0 else out_ref
        ref = arr.at[quarter(h, y)]
        return rcopy(ref, ref, c_ss.at[k, h, 1], c_rs.at[k, h, 1], (((y + i) % NY) * 2 + core, me))

    def half_copy(k, h):
        arr = C2 if k == 0 else out_ref
        ref = arr.at[pl.ds(mine_at[h], RH)]
        return rcopy(ref, ref, c_ss.at[k, h, 0], c_rs.at[k, h, 0], sib)

    def rows_send(k, h):
        for i in (2, 1, 3):
            row_copy(k, h, i).start()

    def rows_pass(k, h):
        arr = C2 if k == 0 else out_ref
        got = arr.at[pl.ds(0, 3 * RQ)]
        rcopy(got, got, c_ss.at[k, h, 1], c_rs.at[k, h, 1], sib).wait_recv()
        half_copy(k, h).start()

    def rows_wait(k, h):
        half_copy(k, h).wait_recv()

    def reduce_drain(it):
        for h in range(CH):
            pair_copy(it, h).wait_send()
            sent = rb2n.at[it, h, pl.ds(1, NY - 1)]
            rcopy(sent, sent, n2_ss.at[it, h], n2_rs.at[it, h], sib).wait_send()
            arr = C2 if it == 0 else out_ref
            sent = arr.at[pl.ds(0, 3 * RQ)]
            rcopy(sent, sent, c_ss.at[it, h, 1], c_rs.at[it, h, 1], sib).wait_send()
            half_copy(it, h).wait_send()

    def early_drain():
        gather_drain()

        def wsq(o, _):
            q_copy(o, dp).wait_send()
            return 0

        lax.fori_loop(1, DP, wsq, 0)

    def mid(it):
        stats_wait(it, NEAR)
        def near(h, _):
            numer(it, h, NEAR)
            return 0

        lax.fori_loop(0, CH, near, 0)
        stats_wait(it, FAR)
        def far(h, _):
            numer(it, h, FAR)
            pair_copy(it, h).start()
            return 0

        lax.fori_loop(0, CH, far, 0)
        for h in range(CH):
            pair_sum(it, h)

    softmax_first()
    owner_combine(0)
    query_post()
    mid(0)
    for h in range(CH):
        newc = update(0, h)
        own[h] = newc
        C2[quarter(h, y), 0:D] = newc.astype(BF16)
        C2[quarter(h, y), D:W] = three(jnp.sum(newc * newc, axis=1, keepdims=True), RQ)
        rows_send(0, h)
    early_drain()
    stats_drain(0)
    for h in range(CH):
        rows_pass(0, h)

    softmax_second()
    owner_combine(1)
    query_finish()
    mid(1)
    for h in range(CH):
        out_ref[quarter(h, y), :] = update(1, h).astype(BF16)
        rows_send(1, h)
    stats_drain(1)
    reduce_drain(0)
    for h in range(CH):
        rows_pass(1, h)
    for h in range(CH):
        rows_wait(1, h)
    reduce_drain(1)


def on_device(passages, queries, init_centroids, pattern, positive_offset):
    vm = pl.BlockSpec(memory_space=pltpu.VMEM)
    anywhere = pl.BlockSpec(memory_space=pl.ANY)
    dma = pltpu.SemaphoreType.DMA
    centroids, loss = pl.pallas_call(
        kernel,
        out_shape=(jax.ShapeDtypeStruct((KL, D), BF16), jax.ShapeDtypeStruct((1, 4), F32)),
        in_specs=[anywhere] * 5,
        out_specs=(vm, vm),
        scratch_shapes=[
            pltpu.VMEM((NZ, NX, BLOCK, D), BF16),
            pltpu.VMEM((NZ, KL, NX * BLOCK), F32),
            pltpu.VMEM((NZ, QP, NX * BLOCK), F32),
            pltpu.VMEM((KL + QP, D), BF16),
            pltpu.VMEM((KL, W), BF16),
            pltpu.VMEM((KL, 128), F32),
            pltpu.VMEM((2, KL, W), F32),
            pltpu.VMEM((2, CH, RH, W), F32),
            pltpu.VMEM((2, CH, RH, W), BF16),
            pltpu.VMEM((2, CH, NY, RQ, W), BF16),
            pltpu.VMEM((CH, RQ, D), F32),
            pltpu.VMEM((KL, D), F32),
            pltpu.VMEM((4, D), BF16),
            pltpu.VMEM((4, 1024), jnp.int32),
            pltpu.VMEM((DP, 128), jnp.int32),
            pltpu.VMEM((5, QP, 128), F32),
            pltpu.VMEM((CENT, 2, 128), F32),
            pltpu.VMEM((2, CENT, 2, 128), F32),
            pltpu.VMEM((2, CENT, 2, 128), F32),
            pltpu.VMEM((8, D), F32),
            pltpu.VMEM((DP, 8, D), F32),
            pltpu.VMEM((DP, 8, 128), F32),
            pltpu.VMEM((DP, 8, 128), F32),
            dma, dma((NZ + 1,)), dma, dma((NZ, 2)),
            dma((2,)), dma((NZ, 4)), dma((4,)), dma((4,)),
            dma((DP,)), dma((DP,)),
            dma((2,)), dma((2,)),
            dma((2,)), dma((2, 2)),
            dma((2, CH)), dma((2, CH)),
            dma((2, CH)), dma((2, CH)),
            dma((2, CH, 2)), dma((2, CH, 2)),
            dma((DP,)), dma((DP,)),
            dma((5,)),
        ],
        compiler_params=pltpu.CompilerParams(
            collective_id=0, has_side_effects=True, vmem_limit_bytes=56 * 1024 * 1024
        ),
    )(passages, queries, init_centroids, pattern.T, positive_offset.reshape(DP, 128))
    return centroids.astype(F32), loss.reshape(4)


def solution(mesh):
    placed = (P(("dp", "cent"), None), P(("dp", "cent"), None), P("cent", None), P(), P())
    return jax.shard_map(
        on_device,
        mesh=mesh,
        in_specs=placed,
        out_specs=(P("cent", None), P(("dp", "cent"))),
        check_vma=False,
    )
```
